32 devices in a mesh: pix: 16 (over z, y, core), frm: 2 (over x).
Axes of the slice: x: 2, y: 2, z: 4, core: 2. Of those that a mesh axis runs over, the one named last changes fastest.
Arguments:
- frames: bfloat16 [65536, 768], P('pix', 'frm'), may hold values from 0 to 6
- footprints: bfloat16 [65536, 192], P('pix'), may hold values from 0 to 0.024414062
- support: int32 [4096, 192], P('pix'), may hold values 0 or 1
- traces: float32 [1024, 768], P('pix', 'frm'), may hold values from 0 to 2
- block_order: int32 [16, 2], replicated, may hold values from 0 to 1, each once within a row
Outputs:
- refined: bfloat16 [65536, 192], P(('pix', 'frm'))
- updated: float32 [1024, 768], P('pix', 'frm')
The draws below stay inside these ranges and needn't reach their ends.
Inputs may be any that keep to these rules, and one draw needn't show every extreme that they name: `block_order`: each row lists every block index of a slab once.
All inputs are finite; a program needn't handle non-finite values. No bound on the sum of `support` on one device may be relied on, other than what follows from the above.
Results may differ from the reference program's by a relative error of at most 0.0036.
Values may be sent and summed in bfloat16 or wider, within the bound.
A program may use at most 64 MiB of HBM per device.

```python
import math
import jax
import jax.numpy as jnp
from jax import lax

KO = 64
BLOCK = 32
TILE = 16
PD = 4096
OWNERS = 16
PIXELS = 65536
TOTAL_FRAMES = 768
K = 1024
B_OWN = 2


def draw_frames(key, part):
    row_key, noise_key = jax.random.split(jax.random.fold_in(key, 7))
    level = jax.random.uniform(row_key, (PIXELS, 1), jnp.float32)
    scale = 0.35 * jnp.exp(level * math.log(8.0))
    noise = jax.random.uniform(noise_key, (PIXELS, TOTAL_FRAMES), jnp.float32, 0.0, 2.0)
    return (scale * noise).astype(jnp.bfloat16)


def with_ends(entries, rng, low, largest):
    index_at = [jax.random.randint(jax.random.fold_in(rng, axis), (), 0, length) for axis, length in enumerate(entries.shape)]
    main_axis = entries.shape.index(max(entries.shape))
    beside = index_at[:main_axis] + [(index_at[main_axis] + 1) % entries.shape[main_axis]] + index_at[main_axis + 1:]
    return entries.at[tuple(index_at)].set(low).at[tuple(beside)].set(largest)


def shard_levels(stream_key, dims, pieces, least, top_value):
    loudness, own = 1.0, jax.random.fold_in(stream_key, 6)
    for position, shards_of in pieces:
        heights = jnp.exp(jax.random.uniform(jax.random.fold_in(own, position), (shards_of,), jnp.float32, least / len(pieces), top_value / len(pieces)))
        loudness = loudness * jnp.repeat(heights, dims[position] // shards_of).reshape([-1 if axis == position else 1 for axis in range(len(dims))])
    return loudness


def setup_inputs(seed: int = 0) -> dict:
    splits = jax.random.split(jax.random.key(seed), 6)
    frames = draw_frames(jax.random.fold_in(splits[5], 71), 0)
    footprints = jnp.clip(0.024414062 * jax.random.uniform(splits[1], (PIXELS, 3 * KO), jnp.float32) ** shard_levels(splits[1], (PIXELS, 3 * KO), ((0, 16),), -0.2, 0.2), 0.0, 0.024414062).astype(jnp.bfloat16)
    support = with_ends((jax.random.randint(splits[2], (PIXELS // TILE, 3 * KO), 0, 2) < 1).astype(jnp.int32), jax.random.fold_in(splits[2], 1), 0, 1)
    traces = jnp.clip(2.0 * jax.random.uniform(splits[3], (K, TOTAL_FRAMES), jnp.float32) ** shard_levels(splits[3], (K, TOTAL_FRAMES), ((0, 16), (1, 2)), -0.2, 0.2), 0.0, 2.0)
    block_order = jax.vmap(lambda own: jax.random.permutation(own, B_OWN))(jax.random.split(splits[4], OWNERS)).reshape((OWNERS, B_OWN)).astype(jnp.int32)
    return {"frames": frames, "footprints": footprints, "support": support, "traces": traces, "block_order": block_order}


highest = lax.Precision.HIGHEST


def slab_masks(support_slab, slab_id):
    expanded = jnp.repeat(support_slab, TILE, axis=0).astype(jnp.float32)
    window_of = jnp.arange(3 * KO, dtype=jnp.int32) // KO
    usable = jnp.where(window_of == 0, slab_id > 0, jnp.where(window_of == 2, slab_id < OWNERS - 1, True))
    return expanded * usable.astype(jnp.float32)[None, :]


def trace_block(current, window, drive_rows, coupling, block_id):
    row_start = (block_id * BLOCK).astype(jnp.int32)
    band_rows = lax.dynamic_slice_in_dim(coupling, row_start, BLOCK, 0)
    diagonal = jnp.diagonal(lax.dynamic_slice_in_dim(band_rows, 2 * KO + row_start, BLOCK, 1))
    product = jnp.dot(band_rows, window, precision=highest)
    target = lax.dynamic_slice_in_dim(drive_rows, row_start, BLOCK, 0)
    before = lax.dynamic_slice_in_dim(current, row_start, BLOCK, 0)
    after = jnp.maximum(before + (target - product) / (diagonal[:, None] + 1.0), 0.0)
    return lax.dynamic_update_slice_in_dim(current, after, row_start, 0)


def reference(frames, footprints, support, traces, block_order):
    frame_slabs = frames.reshape(OWNERS, PD, TOTAL_FRAMES)
    foot_slabs = footprints.reshape(OWNERS, PD, 3 * KO)
    support_slabs = support.reshape(OWNERS, PD // TILE, 3 * KO)
    slab_ids = jnp.arange(OWNERS, dtype=jnp.int32)

    def project(inputs):
        frame_slab, foot_slab, support_slab, slab_id = inputs
        active = (foot_slab.astype(jnp.float32) * slab_masks(support_slab, slab_id)).astype(jnp.bfloat16)
        active_f = active.astype(jnp.float32)
        loads = jnp.einsum("pk,pt->kt", active_f, frame_slab.astype(jnp.float32), precision=highest)
        correlations = jnp.einsum("pk,pj->kj", active_f, active_f, precision=highest)
        return loads, correlations

    loads, correlations = lax.map(project, (frame_slabs, foot_slabs, support_slabs, slab_ids))
    zero_load = jnp.zeros((1, KO, TOTAL_FRAMES), jnp.float32)
    from_right = jnp.concatenate([loads[1:, :KO], zero_load], axis=0)
    from_left = jnp.concatenate([zero_load, loads[:-1, 2 * KO:]], axis=0)
    drive = loads[:, KO:2 * KO] + from_right + from_left
    zero_gram = jnp.zeros((1, KO, 3 * KO), jnp.float32)
    right_rows = jnp.concatenate([correlations[1:, :KO], zero_gram], axis=0)
    left_rows = jnp.concatenate([zero_gram, correlations[:-1, 2 * KO:]], axis=0)
    coupling = jnp.pad(correlations[:, KO:2 * KO], ((0, 0), (0, 0), (KO, KO)))
    coupling = coupling + jnp.pad(right_rows, ((0, 0), (0, 0), (2 * KO, 0)))
    coupling = coupling + jnp.pad(left_rows, ((0, 0), (0, 0), (0, 2 * KO)))

    current = traces.reshape(OWNERS, KO, TOTAL_FRAMES)
    for step in range(B_OWN):
        padded = jnp.pad(current, ((2, 2), (0, 0), (0, 0)))
        windows = jnp.stack([padded[i:i + OWNERS] for i in range(5)], axis=1).reshape(OWNERS, 5 * KO, TOTAL_FRAMES)
        current = jax.vmap(trace_block)(current, windows, drive, coupling, block_order[:, step])

    near_all = jnp.pad(current.astype(jnp.bfloat16), ((1, 1), (0, 0), (0, 0)))

    def refine(inputs):
        frame_slab, foot_slab, support_slab, slab_id = inputs
        near = lax.dynamic_slice_in_dim(near_all, slab_id, 3, 0).reshape(3 * KO, TOTAL_FRAMES).astype(jnp.float32)
        mixing = jnp.einsum("pt,kt->pk", frame_slab.astype(jnp.float32), near, precision=highest)
        gram = jnp.einsum("kt,jt->kj", near, near, precision=highest)
        keep = slab_masks(support_slab, slab_id)
        shaped = foot_slab.astype(jnp.float32) * keep
        for step in range(B_OWN):
            slab_near = jnp.clip(slab_id - 1 + jnp.arange(3, dtype=jnp.int32), 0, OWNERS - 1)
            picked = block_order[slab_near, step]
            columns = (jnp.arange(3, dtype=jnp.int32)[:, None] * KO + picked[:, None] * BLOCK
                       + jnp.arange(BLOCK, dtype=jnp.int32)[None, :]).reshape(-1)
            gram_cols = jnp.take(gram, columns, axis=1)
            diagonal = jnp.diagonal(jnp.take(gram_cols, columns, axis=0))
            before = jnp.take(shaped, columns, axis=1)
            target = jnp.take(mixing, columns, axis=1)
            keep_cols = jnp.take(keep, columns, axis=1)
            product = jnp.dot(shaped, gram_cols, precision=highest)
            after = jnp.maximum(before + (target - product) / (diagonal[None, :] + 1.0), 0.0) * keep_cols
            shaped = shaped.at[:, columns].set(after)
        return shaped.astype(jnp.bfloat16)

    refined = lax.map(refine, (frame_slabs, foot_slabs, support_slabs, slab_ids))
    return refined.reshape(PIXELS, 3 * KO), current.reshape(K, TOTAL_FRAMES)
```

```python
import functools

import jax
import jax.numpy as jnp
from jax import lax
from jax.experimental import pallas as pl
from jax.experimental.pallas import tpu as pltpu
from jax.sharding import PartitionSpec as P

BLOCK = 32
TILE = 16
MESH = pl.DeviceIdType.MESH
SIDES = (-1, 1)
WINDOWS = (1, 0, 2)
WHOLE = 4
f32, bf16 = jnp.float32, jnp.bfloat16
NT = ((1,), (1,))


def dot(a, b, dims=((1,), (0,))):
    return lax.dot_general(a, b, (dims, ((), ())), preferred_element_type=f32)


def halves(x):
    high = x.astype(bf16)
    return high, (x - high.astype(f32)).astype(bf16)


def place(turn, window):
    return (turn * 3 + WINDOWS.index(window)) * BLOCK


def strip(turn, window):
    return pl.ds(place(turn, window), BLOCK)


def product(a, b):
    high, low = halves(b)
    a_high, a_low = halves(a)
    both = dot(jnp.concatenate([a_high, a_low], axis=0), high)
    n = a.shape[0]
    return both[:n] + both[n:] + dot(a_high, low)


def kernel(
    owners, shares, chunks, order_hbm, frames_hbm, foot_hbm, support_hbm, traces_hbm, refined_out, updated_out,
    order_ref, frames_ref, foot_ref, support_ref, traces_ref, act, keep, around, drive, corr, diag_out, diag_in, side_drive,
    after_out, after_in, extra, extra_in, near, near_far, hint_out, hint_in, frames_in, part_out, part_in, mix, shaped,
    in_sem, a_send, a_recv, b_send, b_recv, c_send, c_recv, d_send, d_recv, e_send, e_recv, g_send, g_recv,
    h_send, h_recv, i_send, i_recv, j_send, j_recv, k_send, k_recv, l_send, l_recv,
):
    slab, mine = lax.axis_index("pix"), lax.axis_index("frm")
    pixels, frames_here = frames_ref.shape
    three = act.shape[0]
    half = three // 2
    width = three // 3
    share_rows = pixels // shares
    whole_rows = frames_in.shape[1]
    part_rows = share_rows - whole_rows
    piece = 128
    whole_pieces = whole_rows // piece
    spans, at = [], 0
    for size in chunks:
        spans.append((at, size))
        at += size
    barrier = pltpu.get_barrier_semaphore()

    def present(offset):
        return slab > 0 if offset < 0 else slab < owners - 1

    def partner(d):
        return lax.rem(mine + d, shares)

    for offset in SIDES:
        @pl.when(present(offset))
        def _():
            pl.semaphore_signal(barrier, inc=1, device_id=(slab + offset, mine), device_id_type=MESH)
    for d in range(1, shares):
        pl.semaphore_signal(barrier, inc=1, device_id=(slab, partner(d)), device_id_type=MESH)

    groups = in_sem.shape[0] - 2
    chunk = pixels // groups

    def bring(c):
        rows = pl.ds(c * chunk, chunk)
        return [pltpu.make_async_copy(foot_hbm.at[:, rows], foot_ref.at[:, rows], in_sem.at[c, 0]),
                pltpu.make_async_copy(frames_hbm.at[rows], frames_ref.at[rows], in_sem.at[c, 1])]

    fetch_support = pltpu.make_async_copy(support_hbm, support_ref, in_sem.at[groups, 0])
    fetch_traces = pltpu.make_async_copy(traces_hbm, traces_ref, in_sem.at[groups, 1])
    fetch_order = pltpu.make_async_copy(order_hbm, order_ref, in_sem.at[groups + 1, 0])
    fetch_order.start()
    fetch_traces.start()
    fetch_support.start()
    for c in range(groups):
        for copy in bring(c):
            copy.start()

    def side(offset):
        return 1 if offset < 0 else 0

    for offset in SIDES:
        @pl.when(jnp.logical_not(present(offset)))
        def _():
            here = side(-offset)
            diag_in[here] = jnp.zeros(diag_in.shape[1:], f32)
            side_drive[here] = jnp.zeros(side_drive.shape[1:], f32)
            after_in[here] = jnp.zeros(after_in.shape[1:], f32)
            extra_in[here] = jnp.zeros(extra_in.shape[1:], f32)
            near[strip(1, 1 + offset), :] = jnp.zeros((BLOCK, frames_here), bf16)
            for turn in range(2):
                around[strip(turn, 1 + offset), :] = jnp.zeros((BLOCK, frames_here), f32)
                for d in range(1, shares):
                    near_far[d - 1, strip(turn, 1 + offset), :] = jnp.zeros((BLOCK, frames_here), bf16)

    def remote(src, dst, send, recv, to):
        return pltpu.make_async_remote_copy(
            src_ref=src, dst_ref=dst, send_sem=send, recv_sem=recv, device_id=to, device_id_type=MESH)

    def beside(offset):
        return slab + offset, mine

    def send_traces(turn, offset):
        s = side(offset)
        return remote(around.at[strip(turn, 1)], around.at[strip(turn, 1 - offset)], a_send.at[s, turn], a_recv.at[s, turn],
                      beside(offset))

    def send_diag(offset):
        s = side(offset)
        return remote(diag_out, diag_in.at[s], b_send.at[s], b_recv.at[s], beside(offset))

    def send_drive(turn, offset):
        s = side(offset)
        return remote(drive.at[strip(turn, 1 + offset)], side_drive.at[s, turn], c_send.at[s, turn], c_recv.at[s, turn],
                      beside(offset))

    def send_after(offset):
        s = side(offset)
        return remote(after_out, after_in.at[s], d_send.at[s], d_recv.at[s], beside(offset))

    def send_extra(offset):
        s = side(offset)
        return remote(extra.at[pl.ds(place(0, 1 + offset), BLOCK)], extra_in.at[s], e_send.at[s], e_recv.at[s], beside(offset))

    def send_near(offset):
        s = side(offset)
        return remote(near.at[strip(1, 1)], near.at[strip(1, 1 - offset)], g_send.at[s], g_recv.at[s], beside(offset))

    def send_far(turn, d):
        return remote(near.at[strip(turn, 1)], near_far.at[d - 1, strip(turn, 1)], h_send.at[d - 1, turn], h_recv.at[d - 1, turn],
                      (slab, partner(d)))

    def relay(turn, d, offset):
        s = side(offset)
        return remote(near_far.at[d - 1, strip(turn, 1)], near_far.at[d - 1, strip(turn, 1 - offset)],
                      i_send.at[d - 1, s, turn], i_recv.at[d - 1, s, turn], beside(offset))

    def send_hint(d):
        return remote(hint_out, hint_in.at[d - 1], j_send.at[d - 1], j_recv.at[d - 1], (slab, partner(d)))

    def first_of(who, row):
        return pl.multiple_of(who * share_rows + row, 128)

    def send_frames(d, p):
        return remote(frames_hbm.at[pl.ds(first_of(partner(d), p * piece), piece)], frames_in.at[d - 1, pl.ds(p * piece, piece)],
                      k_send.at[d - 1, p], k_recv.at[d - 1, p], (slab, partner(d)))

    bands = ((0, BLOCK), (BLOCK, 2 * BLOCK), (half, BLOCK), (half + BLOCK, 2 * BLOCK))

    def send_part(d, band, c):
        where = (d - 1, pl.ds(*bands[band]), pl.ds(*spans[c]))
        return remote(part_out.at[where], part_in.at[where], l_send.at[d - 1, band, c], l_recv.at[d - 1, band, c], (slab, partner(d)))

    def start(copy, offset):
        @pl.when(present(offset))
        def _():
            copy(offset).start()

    def arrive(copy, offset):
        @pl.when(present(-offset))
        def _():
            copy(offset).wait_recv()

    def left(copy, offset):
        @pl.when(present(offset))
        def _():
            copy(offset).wait_send()

    def visited(turn, window):
        return order_ref[turn, jnp.clip(slab - 1 + window, 0, owners - 1)]

    def visit(turn, window, low, high):
        in_order = visited(0, window) == 0
        return jnp.where(in_order, low, high) if turn == 0 else jnp.where(in_order, high, low)

    def visit_all(load):
        pairs = {w: (load(w * width), load(w * width + BLOCK)) for w in WINDOWS}
        return [visit(turn, w, *pairs[w]) for turn in range(2) for w in WINDOWS]

    fetch_order.wait()
    fetch_traces.wait()
    for turn in range(2):
        around[strip(turn, 1), :] = visit(turn, 1, traces_ref[:BLOCK, :], traces_ref[BLOCK:, :])

    peers = present(-1).astype(jnp.int32) + present(1).astype(jnp.int32) + shares - 1
    pl.semaphore_wait(barrier, peers)
    for turn in range(2):
        for offset in SIDES:
            start(functools.partial(send_traces, turn), offset)
    for p in range(whole_pieces):
        for d in range(1, shares):
            send_frames(d, p).start()

    usable = {0: (slab > 0).astype(f32), 1: 1.0, 2: (slab < owners - 1).astype(f32)}
    fetch_support.wait()
    supported = jnp.concatenate(visit_all(
        lambda row: support_ref[row : row + BLOCK, :].astype(f32) * usable[row // width]), axis=0).astype(bf16)
    tiles = support_ref.shape[1]
    tile_of = lax.broadcasted_iota(jnp.int32, (tiles, chunk), 1) // TILE
    tile_is = lax.broadcasted_iota(jnp.int32, (tiles, chunk), 0)
    for c in range(groups):
        rows = slice(c * chunk, (c + 1) * chunk)
        spread = (tile_is == tile_of + c * (chunk // TILE)).astype(f32).astype(bf16)
        mask = dot(supported, spread).astype(bf16)
        keep[:, rows] = mask
        from_foot, from_frames = bring(c)
        from_foot.wait()
        active = jnp.concatenate(visit_all(lambda row: foot_ref[row : row + BLOCK, rows]), axis=0) * mask
        act[:, rows] = active
        together = dot(active, active, NT)
        corr[...] = together if c == 0 else corr[...] + together
        from_frames.wait()
        loads = dot(active, frames_ref[rows, :])
        drive[...] = loads if c == 0 else drive[...] + loads

    line = lax.broadcasted_iota(jnp.int32, (three, three), 0)
    column = lax.broadcasted_iota(jnp.int32, (three, three), 1)
    on_diagonal = jnp.where(line == column, corr[...], 0.0)
    diag_out[...] = jnp.broadcast_to(jnp.sum(on_diagonal, axis=0, keepdims=True), diag_out.shape)
    own_diagonal = jnp.sum(on_diagonal, axis=1, keepdims=True)
    for offset in SIDES:
        start(send_diag, offset)

    for turn in range(2):
        for offset in SIDES:
            arrive(functools.partial(send_traces, turn), offset)
    drive[...] -= product(corr[...], around[...])
    for turn in range(2):
        for offset in SIDES:
            start(functools.partial(send_drive, turn), offset)

    for offset in SIDES:
        arrive(send_diag, offset)
    line = lax.broadcasted_iota(jnp.int32, (BLOCK, three), 0)
    column = lax.broadcasted_iota(jnp.int32, (BLOCK, three), 1)
    rates = []
    for turn in range(2):
        diagonal = own_diagonal[place(turn, 1) : place(turn, 1) + BLOCK]
        for offset in SIDES:
            theirs = jnp.where(column == line + place(turn, 1 - offset), diag_in[side(-offset), 0:1, :], 0.0)
            diagonal += jnp.sum(theirs, axis=1, keepdims=True)
        rates.append(1.0 / (diagonal + 1.0))

    before = [around[strip(turn, 1), :] for turn in range(2)]
    for offset in SIDES:
        arrive(functools.partial(send_drive, 0), offset)
    wanted = drive[strip(0, 1), :] + side_drive[0, 0] + side_drive[1, 0]
    after_first = jnp.maximum(before[0] + wanted * rates[0], 0.0)
    after_out[...] = after_first
    for offset in SIDES:
        start(send_after, offset)
    near[strip(0, 1), :] = after_first.astype(bf16)
    for d in range(1, shares):
        send_far(0, d).start()

    ones = jnp.ones((8, frames_here), bf16)

    def hint(known):
        rest = around[known * BLOCK :, :].astype(bf16)
        levels = dot(ones, jnp.concatenate([near[: known * BLOCK, :], rest], axis=0), NT)
        return (levels * (1.0 / frames_here)).astype(bf16)

    def total(rows):
        return jnp.sum(rows.astype(f32), axis=1, keepdims=True)

    def parts(band, level):
        at, size = bands[band]
        known = near[at : at + size, :]
        weight = total(known)
        for c, (begin, length) in enumerate(spans):
            for d in range(1, shares):
                rows = pl.ds(first_of(partner(d), whole_rows + begin), length)
                guess = weight * dot(level, act[:, rows])[0:1]
                part = dot(known, frames_ref[rows, :], NT) - guess
                part_out[d - 1, at : at + size, begin : begin + length] = part.astype(bf16)
                send_part(d, band, c).start()

    level_own = hint(1)
    parts(0, level_own)

    for offset in SIDES:
        arrive(send_after, offset)
    change = jnp.concatenate(
        [after_first - before[0], after_in[0] - around[strip(0, 0), :], after_in[1] - around[strip(0, 2), :]], axis=0)
    extra[...] = -product(corr[half:, :half], change)
    for offset in SIDES:
        start(send_extra, offset)
    near[strip(0, 0), :] = after_in[0].astype(bf16)
    near[strip(0, 2), :] = after_in[1].astype(bf16)
    level_all = hint(3)
    line = lax.broadcasted_iota(jnp.int32, (8, three), 0)
    hint_out[...] = jnp.where(line == 0, level_own.astype(f32), level_all.astype(f32))
    for d in range(1, shares):
        send_hint(d).start()
    parts(1, level_all)

    for d in range(1, shares):
        send_far(0, d).wait_recv()
        for offset in SIDES:
            start(functools.partial(relay, 0, d), offset)

    for offset in SIDES:
        arrive(functools.partial(send_drive, 1), offset)
        arrive(send_extra, offset)
    wanted = drive[strip(1, 1), :] + side_drive[0, 1] + side_drive[1, 1] + extra[0:BLOCK, :] + extra_in[0] + extra_in[1]
    after_second = jnp.maximum(before[1] + wanted * rates[1], 0.0)
    near[strip(1, 1), :] = after_second.astype(bf16)
    for offset in SIDES:
        start(send_near, offset)
    for d in range(1, shares):
        send_far(1, d).start()
    parts(2, level_all)
    for block in range(2):
        updated_out[block * BLOCK : (block + 1) * BLOCK, :] = visit(block, 1, after_first, after_second)
    for offset in SIDES:
        arrive(send_near, offset)
    parts(3, level_all)

    for d in range(1, shares):
        send_far(1, d).wait_recv()
        for offset in SIDES:
            start(functools.partial(relay, 1, d), offset)

    known = near[...]
    regions = [(0, whole_rows)] + [(whole_rows + begin, length) for begin, length in spans]
    for begin, length in regions:
        mix[:, begin : begin + length] = dot(known, frames_ref[pl.ds(first_of(mine, begin), length), :], NT)

    for d in range(1, shares):
        for turn in range(2):
            for offset in SIDES:
                arrive(functools.partial(relay, turn, d), offset)
    gram = dot(known, known, NT)
    for d in range(1, shares):
        gram += dot(near_far[d - 1], near_far[d - 1], NT)
    line = lax.broadcasted_iota(jnp.int32, (three, three), 0)
    column = lax.broadcasted_iota(jnp.int32, (three, three), 1)
    scale = jnp.sum(jnp.where(line == column, gram, 0.0), axis=1, keepdims=True) + 1.0
    rate = 1.0 / scale
    grams = []
    for turn in range(2):
        high, low = halves(gram[turn * half : (turn + 1) * half])
        grams.append((jnp.concatenate([high, low], axis=0), high[:, :half]))

    def step_one(begin, length):
        here, cols = pl.ds(first_of(mine, begin), length), slice(begin, begin + length)
        active = act[:, here]
        fitted = dot(grams[0][0], active)
        left_over = mix[:half, cols] - fitted[:half] - fitted[half:]
        grown = active[:half].astype(f32) + left_over * rate[:half]
        after = jnp.maximum(grown, 0.0) * keep[:half, here].astype(f32)
        high, low = halves(after)
        shaped[:, cols] = high
        fitted = dot(grams[1][0], jnp.concatenate([high, active[half:]], axis=0))
        mix[half:, cols] += active[half:].astype(f32) * scale[half:] - fitted[:half] - fitted[half:] - dot(grams[1][1], low)

    def step_two(begin, length):
        here, cols = pl.ds(first_of(mine, begin), length), slice(begin, begin + length)
        after = jnp.maximum(mix[half:, cols] * rate[half:], 0.0) * keep[half:, here].astype(f32)
        second = after.astype(bf16)
        for window in range(3):
            row = place(0, window)
            for block in range(2):
                out = window * width + block * BLOCK
                refined_out[out : out + BLOCK, cols] = visit(
                    block, window, shaped[row : row + BLOCK, cols], second[row : row + BLOCK])

    for d in range(1, shares):
        for p in range(whole_pieces):
            send_frames(d, p).wait_recv()
        mix[:, :whole_rows] += dot(near_far[d - 1], frames_in[d - 1], NT)
    step_one(0, whole_rows)
    step_two(0, whole_rows)

    for d in range(1, shares):
        send_hint(d).wait_recv()
    weights = [total(near_far[d - 1]) for d in range(1, shares)]
    for c, (begin, length) in enumerate(spans):
        here, cols = pl.ds(first_of(mine, whole_rows + begin), length), slice(whole_rows + begin, whole_rows + begin + length)
        for d in range(1, shares):
            guesses = dot(hint_in[d - 1].astype(bf16), act[:, here])
            send_part(d, 0, c).wait_recv()
            send_part(d, 1, c).wait_recv()
            near_part = part_in[d - 1, :half, begin : begin + length].astype(f32)
            weight = weights[d - 1]
            mix[:BLOCK, cols] += near_part[:BLOCK] + weight[:BLOCK] * guesses[0:1]
            mix[BLOCK:half, cols] += near_part[BLOCK:] + weight[BLOCK:half] * guesses[1:2]
            mix[half:, cols] += weight[half:] * guesses[1:2]
        step_one(whole_rows + begin, length)
    for c, (begin, length) in enumerate(spans):
        cols = slice(whole_rows + begin, whole_rows + begin + length)
        for d in range(1, shares):
            send_part(d, 2, c).wait_recv()
            send_part(d, 3, c).wait_recv()
            mix[half:, cols] += part_in[d - 1, half:, begin : begin + length].astype(f32)
        step_two(whole_rows + begin, length)

    for offset in SIDES:
        for copy in (send_diag, send_after, send_extra, send_near):
            left(copy, offset)
        for turn in range(2):
            left(functools.partial(send_traces, turn), offset)
            left(functools.partial(send_drive, turn), offset)
            for d in range(1, shares):
                left(functools.partial(relay, turn, d), offset)
    for d in range(1, shares):
        send_hint(d).wait_send()
        for turn in range(2):
            send_far(turn, d).wait_send()
        for p in range(whole_pieces):
            send_frames(d, p).wait_send()
        for c in range(len(spans)):
            for band in range(4):
                send_part(d, band, c).wait_send()


def deliver_kernel(refined_ref, updated_ref, refined_out, updated_out, sem):
    rows = refined_ref.shape[0] // 4
    moves = [(updated_ref, updated_out)]
    for i in range(4):
        part = pl.ds(i * rows, rows)
        moves.append((refined_ref.at[part], refined_out.at[part]))
    copies = [pltpu.make_async_copy(a, b, sem.at[i]) for i, (a, b) in enumerate(moves)]
    for copy in copies:
        copy.start()
    for copy in copies:
        copy.wait()


def deliver(refined, updated):
    refined, updated = (pltpu.with_memory_space_constraint(x, pltpu.VMEM) for x in (refined, updated))
    like = [jax.ShapeDtypeStruct(x.shape, x.dtype) for x in (refined, updated)]
    anywhere = pl.BlockSpec(memory_space=pl.ANY)
    refined, updated = pl.pallas_call(
        deliver_kernel, out_shape=like, in_specs=[anywhere] * 2, out_specs=[anywhere] * 2,
        scratch_shapes=[pltpu.SemaphoreType.DMA((5,))],
    )(refined, updated)
    return refined.T, updated


def cut(rows):
    sizes = []
    while rows > 512:
        sizes.append(512)
        rows -= 512
    return sizes + ([rows - 128, 128] if rows > 128 else [rows])


def shards(owners, shares, frames, footprints, support, traces, block_order):
    pixels, frames_here = frames.shape
    width = traces.shape[0]
    three = 3 * width
    share_rows = pixels // shares
    whole_rows = max(share_rows * WHOLE // 16 // 128, 1) * 128
    part_rows = share_rows - whole_rows
    chunks = cut(part_rows)
    others = shares - 1
    groups = 4
    vmem, dma = pltpu.VMEM, pltpu.SemaphoreType.DMA
    refined, updated = pl.pallas_call(
        functools.partial(kernel, owners, shares, chunks),
        out_shape=(pltpu.VMEM((three, share_rows), bf16), pltpu.VMEM(traces.shape, f32)),
        in_specs=[pl.BlockSpec(memory_space=pl.ANY)] * 5,
        out_specs=[pl.BlockSpec(memory_space=pltpu.VMEM)] * 2,
        scratch_shapes=[
            pltpu.SMEM(block_order.shape[::-1], jnp.int32),
            vmem(frames.shape, bf16),
            vmem((three, pixels), bf16),
            vmem(support.shape[::-1], jnp.int32),
            vmem(traces.shape, f32),
            vmem((three, pixels), bf16),
            vmem((three, pixels), bf16),
            vmem((three, frames_here), f32),
            vmem((three, frames_here), f32),
            vmem((three, three), f32),
            vmem((8, three), f32),
            vmem((2, 8, three), f32),
            vmem((2, 2, BLOCK, frames_here), f32),
            vmem((BLOCK, frames_here), f32),
            vmem((2, BLOCK, frames_here), f32),
            vmem((3 * BLOCK, frames_here), f32),
            vmem((2, BLOCK, frames_here), f32),
            vmem((three, frames_here), bf16),
            vmem((others, three, frames_here), bf16),
            vmem((8, three), f32),
            vmem((others, 8, three), f32),
            vmem((others, whole_rows, frames_here), bf16),
            vmem((others, three, part_rows), bf16),
            vmem((others, three, part_rows), bf16),
            vmem((three, share_rows), f32),
            vmem((three // 2, share_rows), bf16),
            dma((groups + 2, 2)),
            dma((2, 2)), dma((2, 2)), dma((2,)), dma((2,)), dma((2, 2)), dma((2, 2)),
            dma((2,)), dma((2,)), dma((2,)), dma((2,)), dma((2,)), dma((2,)),
            dma((others, 2)), dma((others, 2)), dma((others, 2, 2)), dma((others, 2, 2)),
            dma((others,)), dma((others,)),
            dma((others, whole_rows // 128)), dma((others, whole_rows // 128)),
            dma((others, 4, len(chunks))), dma((others, 4, len(chunks))),
        ],
        compiler_params=pltpu.CompilerParams(
            collective_id=0, has_side_effects=True, vmem_limit_bytes=48 * 1024 * 1024
        ),
    )(block_order.T, frames, footprints.T, support.T, traces)
    return deliver(refined, updated)


def solution(mesh):
    in_specs = (P("pix", "frm"), P("pix", None), P("pix", None), P("pix", "frm"), P())
    out_specs = (P(("pix", "frm"), None), P("pix", "frm"))
    body = functools.partial(shards, mesh.shape["pix"], mesh.shape["frm"])
    return jax.shard_map(body, mesh=mesh, in_specs=in_specs, out_specs=out_specs, check_vma=False)
```

```python
import functools

import jax
import jax.numpy as jnp
from jax import lax
from jax.experimental import pallas as pl
from jax.experimental.pallas import tpu as pltpu
from jax.sharding import PartitionSpec as P

BLOCK = 32
TILE = 16
MESH = pl.DeviceIdType.MESH
SIDES = (-1, 1)
WINDOWS = (1, 0, 2)
WHOLE = 4
f32, bf16 = jnp.float32, jnp.bfloat16
NT = ((1,), (1,))


def dot(a, b, dims=((1,), (0,))):
    return lax.dot_general(a, b, (dims, ((), ())), preferred_element_type=f32)


def halves(x):
    high = x.astype(bf16)
    return high, (x - high.astype(f32)).astype(bf16)


def place(turn, window):
    return (turn * 3 + WINDOWS.index(window)) * BLOCK


def strip(turn, window):
    return pl.ds(place(turn, window), BLOCK)


def product(a, b):
    high, low = halves(b)
    a_high, a_low = halves(a)
    both = dot(jnp.concatenate([a_high, a_low], axis=0), high)
    n = a.shape[0]
    return both[:n] + both[n:] + dot(a_high, low)


def kernel(
    owners, shares, chunks, order_hbm, frames_hbm, foot_hbm, support_hbm, traces_hbm, refined_out, updated_out,
    order_ref, frames_ref, foot_ref, support_ref, traces_ref, act, keep, around, drive, corr, diag_out, diag_in, side_drive,
    after_out, after_in, extra, extra_in, near, near_far, hint_out, hint_in, frames_in, part_out, part_in, mix, shaped,
    in_sem, a_send, a_recv, b_send, b_recv, c_send, c_recv, d_send, d_recv, e_send, e_recv, g_send, g_recv,
    h_send, h_recv, i_send, i_recv, j_send, j_recv, k_send, k_recv, l_send, l_recv,
):
    slab, mine = lax.axis_index("pix"), lax.axis_index("frm")
    pixels, frames_here = frames_ref.shape
    three = act.shape[0]
    half = three // 2
    width = three // 3
    share_rows = pixels // shares
    whole_rows = frames_in.shape[1]
    part_rows = share_rows - whole_rows
    piece = 128
    whole_pieces = whole_rows // piece
    spans, at = [], 0
    for size in chunks:
        spans.append((at, size))
        at += size
    barrier = pltpu.get_barrier_semaphore()

    def present(offset):
        return slab > 0 if offset < 0 else slab < owners - 1

    def partner(d):
        return lax.rem(mine + d, shares)

    for offset in SIDES:
        @pl.when(present(offset))
        def _():
            pl.semaphore_signal(barrier, inc=1, device_id=(slab + offset, mine), device_id_type=MESH)
    for d in range(1, shares):
        pl.semaphore_signal(barrier, inc=1, device_id=(slab, partner(d)), device_id_type=MESH)

    groups = in_sem.shape[0] - 2
    chunk = pixels // groups

    def bring(c):
        rows = pl.ds(c * chunk, chunk)
        return [pltpu.make_async_copy(foot_hbm.at[:, rows], foot_ref.at[:, rows], in_sem.at[c, 0]),
                pltpu.make_async_copy(frames_hbm.at[rows], frames_ref.at[rows], in_sem.at[c, 1])]

    fetch_support = pltpu.make_async_copy(support_hbm, support_ref, in_sem.at[groups, 0])
    fetch_traces = pltpu.make_async_copy(traces_hbm, traces_ref, in_sem.at[groups, 1])
    fetch_order = pltpu.make_async_copy(order_hbm, order_ref, in_sem.at[groups + 1, 0])
    fetch_order.start()
    fetch_traces.start()
    fetch_support.start()
    for c in range(groups):
        for copy in bring(c):
            copy.start()

    def side(offset):
        return 1 if offset < 0 else 0

    for offset in SIDES:
        @pl.when(jnp.logical_not(present(offset)))
        def _():
            here = side(-offset)
            diag_in[here] = jnp.zeros(diag_in.shape[1:], f32)
            side_drive[here] = jnp.zeros(side_drive.shape[1:], f32)
            after_in[here] = jnp.zeros(after_in.shape[1:], f32)
            extra_in[here] = jnp.zeros(extra_in.shape[1:], f32)
            near[strip(1, 1 + offset), :] = jnp.zeros((BLOCK, frames_here), bf16)
            for turn in range(2):
                around[strip(turn, 1 + offset), :] = jnp.zeros((BLOCK, frames_here), f32)
                for d in range(1, shares):
                    near_far[d - 1, strip(turn, 1 + offset), :] = jnp.zeros((BLOCK, frames_here), bf16)

    def remote(src, dst, send, recv, to):
        return pltpu.make_async_remote_copy(
            src_ref=src, dst_ref=dst, send_sem=send, recv_sem=recv, device_id=to, device_id_type=MESH)

    def beside(offset):
        return slab + offset, mine

    def send_traces(turn, offset):
        s = side(offset)
        return remote(around.at[strip(turn, 1)], around.at[strip(turn, 1 - offset)], a_send.at[s, turn], a_recv.at[s, turn],
                      beside(offset))

    def send_diag(offset):
        s = side(offset)
        return remote(diag_out, diag_in.at[s], b_send.at[s], b_recv.at[s], beside(offset))

    def send_drive(turn, offset):
        s = side(offset)
        return remote(drive.at[strip(turn, 1 + offset)], side_drive.at[s, turn], c_send.at[s, turn], c_recv.at[s, turn],
                      beside(offset))

    def send_after(offset):
        s = side(offset)
        return remote(after_out, after_in.at[s], d_send.at[s], d_recv.at[s], beside(offset))

    def send_extra(offset):
        s = side(offset)
        return remote(extra.at[pl.ds(place(0, 1 + offset), BLOCK)], extra_in.at[s], e_send.at[s], e_recv.at[s], beside(offset))

    def send_near(offset):
        s = side(offset)
        return remote(near.at[strip(1, 1)], near.at[strip(1, 1 - offset)], g_send.at[s], g_recv.at[s], beside(offset))

    def send_far(turn, d):
        return remote(near.at[strip(turn, 1)], near_far.at[d - 1, strip(turn, 1)], h_send.at[d - 1, turn], h_recv.at[d - 1, turn],
                      (slab, partner(d)))

    def relay(turn, d, offset):
        s = side(offset)
        return remote(near_far.at[d - 1, strip(turn, 1)], near_far.at[d - 1, strip(turn, 1 - offset)],
                      i_send.at[d - 1, s, turn], i_recv.at[d - 1, s, turn], beside(offset))

    def send_hint(d):
        return remote(hint_out, hint_in.at[d - 1], j_send.at[d - 1], j_recv.at[d - 1], (slab, partner(d)))

    def first_of(who, row):
        return pl.multiple_of(who * share_rows + row, 128)

    def send_frames(d, p):
        return remote(frames_hbm.at[pl.ds(first_of(partner(d), p * piece), piece)], frames_in.at[d - 1, pl.ds(p * piece, piece)],
                      k_send.at[d - 1, p], k_recv.at[d - 1, p], (slab, partner(d)))

    bands = ((0, BLOCK), (BLOCK, 2 * BLOCK), (half, BLOCK), (half + BLOCK, 2 * BLOCK))

    def send_part(d, band, c):
        where = (d - 1, pl.ds(*bands[band]), pl.ds(*spans[c]))
        return remote(part_out.at[where], part_in.at[where], l_send.at[d - 1, band, c], l_recv.at[d - 1, band, c], (slab, partner(d)))

    def start(copy, offset):
        @pl.when(present(offset))
        def _():
            copy(offset).start()

    def arrive(copy, offset):
        @pl.when(present(-offset))
        def _():
            copy(offset).wait_recv()

    def left(copy, offset):
        @pl.when(present(offset))
        def _():
            copy(offset).wait_send()

    def visited(turn, window):
        return order_ref[turn, jnp.clip(slab - 1 + window, 0, owners - 1)]

    def visit(turn, window, low, high):
        in_order = visited(0, window) == 0
        return jnp.where(in_order, low, high) if turn == 0 else jnp.where(in_order, high, low)

    def visit_all(load):
        pairs = {w: (load(w * width), load(w * width + BLOCK)) for w in WINDOWS}
        return [visit(turn, w, *pairs[w]) for turn in range(2) for w in WINDOWS]

    fetch_order.wait()
    fetch_traces.wait()
    for turn in range(2):
        around[strip(turn, 1), :] = visit(turn, 1, traces_ref[:BLOCK, :], traces_ref[BLOCK:, :])

    usable = {0: (slab > 0).astype(f32), 1: 1.0, 2: (slab < owners - 1).astype(f32)}
    fetch_support.wait()
    supported = jnp.concatenate(visit_all(
        lambda row: support_ref[row : row + BLOCK, :].astype(f32) * usable[row // width]), axis=0).astype(bf16)
    tiles = support_ref.shape[1]
    stretch = pixels // 4
    tile_of = lax.broadcasted_iota(jnp.int32, (tiles, stretch), 1) // TILE
    tile_is = lax.broadcasted_iota(jnp.int32, (tiles, stretch), 0)
    for c in range(4):
        spread = (tile_is == tile_of + c * (stretch // TILE)).astype(f32).astype(bf16)
        keep[:, c * stretch : (c + 1) * stretch] = dot(supported, spread).astype(bf16)

    peers = present(-1).astype(jnp.int32) + present(1).astype(jnp.int32) + shares - 1
    pl.semaphore_wait(barrier, peers)
    for turn in range(2):
        for offset in SIDES:
            start(functools.partial(send_traces, turn), offset)
    for p in range(whole_pieces):
        for d in range(1, shares):
            send_frames(d, p).start()

    for c in range(groups):
        rows = slice(c * chunk, (c + 1) * chunk)
        for copy in bring(c):
            copy.wait()
        active = jnp.concatenate(visit_all(lambda row: foot_ref[row : row + BLOCK, rows]), axis=0) * keep[:, rows]
        act[:, rows] = active
        together = dot(active, active, NT)
        corr[...] = together if c == 0 else corr[...] + together
        loads = dot(active, frames_ref[rows, :])
        drive[...] = loads if c == 0 else drive[...] + loads

    line = lax.broadcasted_iota(jnp.int32, (three, three), 0)
    column = lax.broadcasted_iota(jnp.int32, (three, three), 1)
    on_diagonal = jnp.where(line == column, corr[...], 0.0)
    diag_out[...] = jnp.broadcast_to(jnp.sum(on_diagonal, axis=0, keepdims=True), diag_out.shape)
    own_diagonal = jnp.sum(on_diagonal, axis=1, keepdims=True)
    for offset in SIDES:
        start(send_diag, offset)

    for turn in range(2):
        for offset in SIDES:
            arrive(functools.partial(send_traces, turn), offset)
    drive[...] -= product(corr[...], around[...])
    for turn in range(2):
        for offset in SIDES:
            start(functools.partial(send_drive, turn), offset)

    for offset in SIDES:
        arrive(send_diag, offset)
    line = lax.broadcasted_iota(jnp.int32, (BLOCK, three), 0)
    column = lax.broadcasted_iota(jnp.int32, (BLOCK, three), 1)
    rates = []
    for turn in range(2):
        diagonal = own_diagonal[place(turn, 1) : place(turn, 1) + BLOCK]
        for offset in SIDES:
            theirs = jnp.where(column == line + place(turn, 1 - offset), diag_in[side(-offset), 0:1, :], 0.0)
            diagonal += jnp.sum(theirs, axis=1, keepdims=True)
        rates.append(1.0 / (diagonal + 1.0))

    before = [around[strip(turn, 1), :] for turn in range(2)]
    for offset in SIDES:
        arrive(functools.partial(send_drive, 0), offset)
    wanted = drive[strip(0, 1), :] + side_drive[0, 0] + side_drive[1, 0]
    after_first = jnp.maximum(before[0] + wanted * rates[0], 0.0)
    after_out[...] = after_first
    for offset in SIDES:
        start(send_after, offset)
    near[strip(0, 1), :] = after_first.astype(bf16)
    for d in range(1, shares):
        send_far(0, d).start()

    ones = jnp.ones((8, frames_here), bf16)

    def hint(known):
        rest = around[known * BLOCK :, :].astype(bf16)
        levels = dot(ones, jnp.concatenate([near[: known * BLOCK, :], rest], axis=0), NT)
        return (levels * (1.0 / frames_here)).astype(bf16)

    def total(rows):
        return jnp.sum(rows.astype(f32), axis=1, keepdims=True)

    def parts(band, level):
        at, size = bands[band]
        known = near[at : at + size, :]
        weight = total(known)
        for c, (begin, length) in enumerate(spans):
            for d in range(1, shares):
                rows = pl.ds(first_of(partner(d), whole_rows + begin), length)
                guess = weight * dot(level, act[:, rows])[0:1]
                part = dot(known, frames_ref[rows, :], NT) - guess
                part_out[d - 1, at : at + size, begin : begin + length] = part.astype(bf16)
                send_part(d, band, c).start()

    level_own = hint(1)
    parts(0, level_own)

    for offset in SIDES:
        arrive(send_after, offset)
    change = jnp.concatenate(
        [after_first - before[0], after_in[0] - around[strip(0, 0), :], after_in[1] - around[strip(0, 2), :]], axis=0)
    extra[...] = -product(corr[half:, :half], change)
    for offset in SIDES:
        start(send_extra, offset)
    near[strip(0, 0), :] = after_in[0].astype(bf16)
    near[strip(0, 2), :] = after_in[1].astype(bf16)
    level_all = hint(3)
    line = lax.broadcasted_iota(jnp.int32, (8, three), 0)
    hint_out[...] = jnp.where(line == 0, level_own.astype(f32), level_all.astype(f32))
    for d in range(1, shares):
        send_hint(d).start()
    parts(1, level_all)

    for d in range(1, shares):
        send_far(0, d).wait_recv()
        for offset in SIDES:
            start(functools.partial(relay, 0, d), offset)

    for offset in SIDES:
        arrive(functools.partial(send_drive, 1), offset)
        arrive(send_extra, offset)
    wanted = drive[strip(1, 1), :] + side_drive[0, 1] + side_drive[1, 1] + extra[0:BLOCK, :] + extra_in[0] + extra_in[1]
    after_second = jnp.maximum(before[1] + wanted * rates[1], 0.0)
    near[strip(1, 1), :] = after_second.astype(bf16)
    for offset in SIDES:
        start(send_near, offset)
    for d in range(1, shares):
        send_far(1, d).start()
    parts(2, level_all)
    for block in range(2):
        updated_out[block * BLOCK : (block + 1) * BLOCK, :] = visit(block, 1, after_first, after_second)
    for offset in SIDES:
        arrive(send_near, offset)
    parts(3, level_all)

    for d in range(1, shares):
        send_far(1, d).wait_recv()
        for offset in SIDES:
            start(functools.partial(relay, 1, d), offset)

    known = near[...]
    regions = [(0, whole_rows)] + [(whole_rows + begin, length) for begin, length in spans]
    for begin, length in regions:
        mix[:, begin : begin + length] = dot(known, frames_ref[pl.ds(first_of(mine, begin), length), :], NT)

    for d in range(1, shares):
        for turn in range(2):
            for offset in SIDES:
                arrive(functools.partial(relay, turn, d), offset)
    gram = dot(known, known, NT)
    for d in range(1, shares):
        gram += dot(near_far[d - 1], near_far[d - 1], NT)
    line = lax.broadcasted_iota(jnp.int32, (three, three), 0)
    column = lax.broadcasted_iota(jnp.int32, (three, three), 1)
    scale = jnp.sum(jnp.where(line == column, gram, 0.0), axis=1, keepdims=True) + 1.0
    rate = 1.0 / scale
    grams = []
    for turn in range(2):
        high, low = halves(gram[turn * half : (turn + 1) * half])
        grams.append((jnp.concatenate([high, low], axis=0), high[:, :half]))

    def step_one(begin, length):
        here, cols = pl.ds(first_of(mine, begin), length), slice(begin, begin + length)
        active = act[:, here]
        fitted = dot(grams[0][0], active)
        left_over = mix[:half, cols] - fitted[:half] - fitted[half:]
        grown = active[:half].astype(f32) + left_over * rate[:half]
        after = jnp.maximum(grown, 0.0) * keep[:half, here].astype(f32)
        high, low = halves(after)
        shaped[:, cols] = high
        fitted = dot(grams[1][0], jnp.concatenate([high, active[half:]], axis=0))
        mix[half:, cols] += active[half:].astype(f32) * scale[half:] - fitted[:half] - fitted[half:] - dot(grams[1][1], low)

    def step_two(begin, length):
        here, cols = pl.ds(first_of(mine, begin), length), slice(begin, begin + length)
        after = jnp.maximum(mix[half:, cols] * rate[half:], 0.0) * keep[half:, here].astype(f32)
        second = after.astype(bf16)
        for window in range(3):
            row = place(0, window)
            for block in range(2):
                out = window * width + block * BLOCK
                refined_out[out : out + BLOCK, cols] = visit(
                    block, window, shaped[row : row + BLOCK, cols], second[row : row + BLOCK])

    for d in range(1, shares):
        for p in range(whole_pieces):
            send_frames(d, p).wait_recv()
        mix[:, :whole_rows] += dot(near_far[d - 1], frames_in[d - 1], NT)
    step_one(0, whole_rows)
    step_two(0, whole_rows)

    for d in range(1, shares):
        send_hint(d).wait_recv()
    weights = [total(near_far[d - 1]) for d in range(1, shares)]
    for c, (begin, length) in enumerate(spans):
        here, cols = pl.ds(first_of(mine, whole_rows + begin), length), slice(whole_rows + begin, whole_rows + begin + length)
        for d in range(1, shares):
            guesses = dot(hint_in[d - 1].astype(bf16), act[:, here])
            send_part(d, 0, c).wait_recv()
            send_part(d, 1, c).wait_recv()
            near_part = part_in[d - 1, :half, begin : begin + length].astype(f32)
            weight = weights[d - 1]
            mix[:BLOCK, cols] += near_part[:BLOCK] + weight[:BLOCK] * guesses[0:1]
            mix[BLOCK:half, cols] += near_part[BLOCK:] + weight[BLOCK:half] * guesses[1:2]
            mix[half:, cols] += weight[half:] * guesses[1:2]
        step_one(whole_rows + begin, length)
    for c, (begin, length) in enumerate(spans):
        cols = slice(whole_rows + begin, whole_rows + begin + length)
        for d in range(1, shares):
            send_part(d, 2, c).wait_recv()
            send_part(d, 3, c).wait_recv()
            mix[half:, cols] += part_in[d - 1, half:, begin : begin + length].astype(f32)
        step_two(whole_rows + begin, length)

    for offset in SIDES:
        for copy in (send_diag, send_after, send_extra, send_near):
            left(copy, offset)
        for turn in range(2):
            left(functools.partial(send_traces, turn), offset)
            left(functools.partial(send_drive, turn), offset)
            for d in range(1, shares):
                left(functools.partial(relay, turn, d), offset)
    for d in range(1, shares):
        send_hint(d).wait_send()
        for turn in range(2):
            send_far(turn, d).wait_send()
        for p in range(whole_pieces):
            send_frames(d, p).wait_send()
        for c in range(len(spans)):
            for band in range(4):
                send_part(d, band, c).wait_send()


def deliver_kernel(refined_ref, updated_ref, refined_out, updated_out, sem):
    rows = refined_ref.shape[0] // 4
    moves = [(updated_ref, updated_out)]
    for i in range(4):
        part = pl.ds(i * rows, rows)
        moves.append((refined_ref.at[part], refined_out.at[part]))
    copies = [pltpu.make_async_copy(a, b, sem.at[i]) for i, (a, b) in enumerate(moves)]
    for copy in copies:
        copy.start()
    for copy in copies:
        copy.wait()


def deliver(refined, updated):
    refined, updated = (pltpu.with_memory_space_constraint(x, pltpu.VMEM) for x in (refined, updated))
    like = [jax.ShapeDtypeStruct(x.shape, x.dtype) for x in (refined, updated)]
    anywhere = pl.BlockSpec(memory_space=pl.ANY)
    refined, updated = pl.pallas_call(
        deliver_kernel, out_shape=like, in_specs=[anywhere] * 2, out_specs=[anywhere] * 2,
        scratch_shapes=[pltpu.SemaphoreType.DMA((5,))],
    )(refined, updated)
    return refined.T, updated


def cut(rows):
    sizes = []
    while rows > 512:
        sizes.append(512)
        rows -= 512
    return sizes + ([rows - 128, 128] if rows > 128 else [rows])


def shards(owners, shares, frames, footprints, support, traces, block_order):
    pixels, frames_here = frames.shape
    width = traces.shape[0]
    three = 3 * width
    share_rows = pixels // shares
    whole_rows = max(share_rows * WHOLE // 16 // 128, 1) * 128
    part_rows = share_rows - whole_rows
    chunks = cut(part_rows)
    others = shares - 1
    groups = 2
    vmem, dma = pltpu.VMEM, pltpu.SemaphoreType.DMA
    refined, updated = pl.pallas_call(
        functools.partial(kernel, owners, shares, chunks),
        out_shape=(pltpu.VMEM((three, share_rows), bf16), pltpu.VMEM(traces.shape, f32)),
        in_specs=[pl.BlockSpec(memory_space=pltpu.HBM)] * 5,
        out_specs=[pl.BlockSpec(memory_space=pltpu.VMEM)] * 2,
        scratch_shapes=[
            pltpu.SMEM(block_order.shape[::-1], jnp.int32),
            vmem(frames.shape, bf16),
            vmem((three, pixels), bf16),
            vmem(support.shape[::-1], jnp.int32),
            vmem(traces.shape, f32),
            vmem((three, pixels), bf16),
            vmem((three, pixels), bf16),
            vmem((three, frames_here), f32),
            vmem((three, frames_here), f32),
            vmem((three, three), f32),
            vmem((8, three), f32),
            vmem((2, 8, three), f32),
            vmem((2, 2, BLOCK, frames_here), f32),
            vmem((BLOCK, frames_here), f32),
            vmem((2, BLOCK, frames_here), f32),
            vmem((3 * BLOCK, frames_here), f32),
            vmem((2, BLOCK, frames_here), f32),
            vmem((three, frames_here), bf16),
            vmem((others, three, frames_here), bf16),
            vmem((8, three), f32),
            vmem((others, 8, three), f32),
            vmem((others, whole_rows, frames_here), bf16),
            vmem((others, three, part_rows), bf16),
            vmem((others, three, part_rows), bf16),
            vmem((three, share_rows), f32),
            vmem((three // 2, share_rows), bf16),
            dma((groups + 2, 2)),
            dma((2, 2)), dma((2, 2)), dma((2,)), dma((2,)), dma((2, 2)), dma((2, 2)),
            dma((2,)), dma((2,)), dma((2,)), dma((2,)), dma((2,)), dma((2,)),
            dma((others, 2)), dma((others, 2)), dma((others, 2, 2)), dma((others, 2, 2)),
            dma((others,)), dma((others,)),
            dma((others, whole_rows // 128)), dma((others, whole_rows // 128)),
            dma((others, 4, len(chunks))), dma((others, 4, len(chunks))),
        ],
        compiler_params=pltpu.CompilerParams(
            collective_id=0, has_side_effects=True, vmem_limit_bytes=56 * 1024 * 1024
        ),
    )(block_order.T, frames, footprints.T, support.T, traces)
    return deliver(refined, updated)


def solution(mesh):
    in_specs = (P("pix", "frm"), P("pix", None), P("pix", None), P("pix", "frm"), P())
    out_specs = (P(("pix", "frm"), None), P("pix", "frm"))
    body = functools.partial(shards, mesh.shape["pix"], mesh.shape["frm"])
    return jax.shard_map(body, mesh=mesh, in_specs=in_specs, out_specs=out_specs, check_vma=False)
```

```python
import functools

import jax
import jax.numpy as jnp
from jax import lax
from jax.experimental import pallas as pl
from jax.experimental.pallas import tpu as pltpu
from jax.sharding import PartitionSpec as P

BLOCK = 32
TILE = 16
MESH = pl.DeviceIdType.MESH
SIDES = (-1, 1)
WINDOWS = (1, 0, 2)
WHOLE = 4
f32, bf16 = jnp.float32, jnp.bfloat16
NT = ((1,), (1,))


def dot(a, b, dims=((1,), (0,))):
    return lax.dot_general(a, b, (dims, ((), ())), preferred_element_type=f32)


def halves(x):
    high = x.astype(bf16)
    return high, (x - high.astype(f32)).astype(bf16)


def place(turn, window):
    return (turn * 3 + WINDOWS.index(window)) * BLOCK


def strip(turn, window):
    return pl.ds(place(turn, window), BLOCK)


def product(a, b):
    (a_high, a_low), (high, low) = a, b
    both = dot(jnp.concatenate([a_high, a_low], axis=0), high)
    n = a_high.shape[0]
    return both[:n] + both[n:] + dot(a_high, low)


def kernel(
    owners, shares, chunks, order_hbm, frames_hbm, foot_hbm, support_hbm, traces_hbm, refined_out, updated_out,
    order_ref, frames_ref, foot_ref, support_ref, traces_ref, act, keep, around, drive, corr, diag_out, diag_in, side_drive,
    rest_out, rest_in, extra, extra_in, near, near_far, guess, hint_out, hint_in, frames_in, part_out, part_in, mix, shaped,
    in_sem, a_send, a_recv, b_send, b_recv, c_send, c_recv, d_send, d_recv, e_send, e_recv, g_send, g_recv,
    h_send, h_recv, i_send, i_recv, j_send, j_recv, k_send, k_recv, l_send, l_recv,
):
    slab, mine = lax.axis_index("pix"), lax.axis_index("frm")
    pixels, frames_here = frames_ref.shape
    three = act.shape[0]
    half = three // 2
    width = three // 3
    share_rows = pixels // shares
    whole_rows = frames_in.shape[1]
    part_rows = share_rows - whole_rows
    whole_pieces = k_send.shape[1]
    piece = whole_rows // whole_pieces
    spans = [[(sum(sizes[:i]), size) for i, size in enumerate(sizes)] for sizes in chunks]
    barrier = pltpu.get_barrier_semaphore()

    def present(offset):
        return slab > 0 if offset < 0 else slab < owners - 1

    def partner(d):
        return lax.rem(mine + d, shares)

    for offset in SIDES:
        @pl.when(present(offset))
        def _():
            pl.semaphore_signal(barrier, inc=1, device_id=(slab + offset, mine), device_id_type=MESH)
    for d in range(1, shares):
        pl.semaphore_signal(barrier, inc=1, device_id=(slab, partner(d)), device_id_type=MESH)

    groups = in_sem.shape[0] - 2
    chunk = pixels // groups

    def bring(c):
        rows = pl.ds(c * chunk, chunk)
        return [pltpu.make_async_copy(foot_hbm.at[:, rows], foot_ref.at[:, rows], in_sem.at[c, 0]),
                pltpu.make_async_copy(frames_hbm.at[rows], frames_ref.at[rows], in_sem.at[c, 1])]

    fetch_support = pltpu.make_async_copy(support_hbm, support_ref, in_sem.at[groups, 0])
    fetch_traces = pltpu.make_async_copy(traces_hbm, traces_ref.at[1], in_sem.at[groups, 1])
    fetch_order = pltpu.make_async_copy(order_hbm, order_ref, in_sem.at[groups + 1, 0])
    fetch_support.start()
    fetch_order.start()
    for c in range(groups):
        for copy in bring(c):
            copy.start()
    fetch_traces.start()

    def side(offset):
        return 1 if offset < 0 else 0

    for offset in SIDES:
        @pl.when(jnp.logical_not(present(offset)))
        def _():
            here = side(-offset)
            diag_in[here] = jnp.zeros(diag_in.shape[1:], f32)
            side_drive[here] = jnp.zeros(side_drive.shape[1:], f32)
            rest_in[here] = jnp.zeros(rest_in.shape[1:], bf16)
            extra_in[here] = jnp.zeros(extra_in.shape[1:], f32)
            traces_ref[1 + offset] = jnp.zeros(traces_ref.shape[1:], f32)
            for turn in range(2):
                near[strip(turn, 1 + offset), :] = jnp.zeros((BLOCK, frames_here), bf16)
                for d in range(1, shares):
                    near_far[d - 1, strip(turn, 1 + offset), :] = jnp.zeros((BLOCK, frames_here), bf16)

    def remote(src, dst, send, recv, to):
        return pltpu.make_async_remote_copy(
            src_ref=src, dst_ref=dst, send_sem=send, recv_sem=recv, device_id=to, device_id_type=MESH)

    def beside(offset):
        return slab + offset, mine

    def send_traces(offset):
        s = side(offset)
        return remote(traces_hbm, traces_ref.at[1 - offset], a_send.at[s], a_recv.at[s], beside(offset))

    def send_diag(offset):
        s = side(offset)
        return remote(diag_out, diag_in.at[s], b_send.at[s], b_recv.at[s], beside(offset))

    def send_drive(turn, offset):
        s = side(offset)
        return remote(drive.at[strip(turn, 1 + offset)], side_drive.at[s, turn], c_send.at[s, turn], c_recv.at[s, turn],
                      beside(offset))

    def send_rest(offset):
        s = side(offset)
        return remote(rest_out, rest_in.at[s], d_send.at[s], d_recv.at[s], beside(offset))

    def send_extra(offset):
        s = side(offset)
        return remote(extra.at[pl.ds(place(0, 1 + offset), BLOCK)], extra_in.at[s], e_send.at[s], e_recv.at[s], beside(offset))

    def send_near(turn, offset):
        s = side(offset)
        return remote(near.at[strip(turn, 1)], near.at[strip(turn, 1 - offset)], g_send.at[s, turn], g_recv.at[s, turn],
                      beside(offset))

    def send_far(turn, d):
        return remote(near.at[strip(turn, 1)], near_far.at[d - 1, strip(turn, 1)], h_send.at[d - 1, turn], h_recv.at[d - 1, turn],
                      (slab, partner(d)))

    def relay(turn, d, offset):
        s = side(offset)
        return remote(near_far.at[d - 1, strip(turn, 1)], near_far.at[d - 1, strip(turn, 1 - offset)],
                      i_send.at[d - 1, s, turn], i_recv.at[d - 1, s, turn], beside(offset))

    def send_hint(d):
        return remote(hint_out, hint_in.at[d - 1], j_send.at[d - 1], j_recv.at[d - 1], (slab, partner(d)))

    def first_of(who, row):
        return pl.multiple_of(who * share_rows + row, 128)

    def send_frames(d, p):
        return remote(frames_hbm.at[pl.ds(first_of(partner(d), p * piece), piece)], frames_in.at[d - 1, pl.ds(p * piece, piece)],
                      k_send.at[d - 1, p], k_recv.at[d - 1, p], (slab, partner(d)))

    bands = ((0, BLOCK), (BLOCK, 2 * BLOCK), (half, BLOCK), (half + BLOCK, 2 * BLOCK))

    def send_part(d, band, c):
        where = (d - 1, pl.ds(*bands[band]), pl.ds(*spans[band][c]))
        return remote(part_out.at[where], part_in.at[where], l_send.at[d - 1, band, c], l_recv.at[d - 1, band, c], (slab, partner(d)))

    def start(copy, offset):
        @pl.when(present(offset))
        def _():
            copy(offset).start()

    def arrive(copy, offset):
        @pl.when(present(-offset))
        def _():
            copy(offset).wait_recv()

    def left(copy, offset):
        @pl.when(present(offset))
        def _():
            copy(offset).wait_send()

    def visited(turn, window):
        return order_ref[turn, jnp.clip(slab - 1 + window, 0, owners - 1)]

    def visit(turn, window, low, high):
        in_order = visited(0, window) == 0
        return jnp.where(in_order, low, high) if turn == 0 else jnp.where(in_order, high, low)

    def visit_all(load):
        pairs = {w: (load(w * width), load(w * width + BLOCK)) for w in WINDOWS}
        return [visit(turn, w, *pairs[w]) for turn in range(2) for w in WINDOWS]

    peers = present(-1).astype(jnp.int32) + present(1).astype(jnp.int32) + shares - 1
    pl.semaphore_wait(barrier, peers)
    for offset in SIDES:
        start(send_traces, offset)
    for p in range(whole_pieces):
        for d in range(1, shares):
            send_frames(d, p).start()

    usable = {0: (slab > 0).astype(f32), 1: 1.0, 2: (slab < owners - 1).astype(f32)}
    fetch_order.wait()
    fetch_support.wait()
    supported = jnp.concatenate(visit_all(
        lambda row: support_ref[row : row + BLOCK, :].astype(f32) * usable[row // width]), axis=0).astype(bf16)
    tiles = support_ref.shape[1]
    stretch = pixels // 4
    tile_of = lax.broadcasted_iota(jnp.int32, (tiles, stretch), 1) // TILE
    tile_is = lax.broadcasted_iota(jnp.int32, (tiles, stretch), 0)
    for c in range(4):
        spread = (tile_is == tile_of + c * (stretch // TILE)).astype(f32).astype(bf16)
        keep[:, c * stretch : (c + 1) * stretch] = dot(supported, spread).astype(bf16)

    for c in range(groups):
        rows = slice(c * chunk, (c + 1) * chunk)
        for copy in bring(c):
            copy.wait()
        active = jnp.concatenate(visit_all(lambda row: foot_ref[row : row + BLOCK, rows]), axis=0) * keep[:, rows]
        act[:, rows] = active
        together = dot(active, active, NT)
        corr[...] = together if c == 0 else corr[...] + together
        loads = dot(active, frames_ref[rows, :])
        drive[...] = loads if c == 0 else drive[...] + loads

    line = lax.broadcasted_iota(jnp.int32, (three, three), 0)
    column = lax.broadcasted_iota(jnp.int32, (three, three), 1)
    on_diagonal = jnp.where(line == column, corr[...], 0.0)
    diag_out[...] = jnp.broadcast_to(jnp.sum(on_diagonal, axis=0, keepdims=True), diag_out.shape)
    own_diagonal = jnp.sum(on_diagonal, axis=1, keepdims=True)
    for offset in SIDES:
        start(send_diag, offset)

    sides, rest = slice(BLOCK, half), [slice(0, BLOCK), slice(half, three)]
    corr_sides = halves(corr[sides, :])
    corr_rest = halves(jnp.concatenate([corr[r, :] for r in rest], axis=0))
    fetch_traces.wait()
    for offset in SIDES:
        arrive(send_traces, offset)
    for turn in range(2):
        for window in WINDOWS:
            around[strip(turn, window), :] = visit(turn, window, traces_ref[window, :BLOCK, :], traces_ref[window, BLOCK:, :])
    spread = halves(around[...])
    drive[sides, :] -= product(corr_sides, spread)
    for offset in SIDES:
        start(functools.partial(send_drive, 0), offset)
    fitted = product(corr_rest, spread)
    drive[rest[0], :] -= fitted[:BLOCK]
    drive[rest[1], :] -= fitted[BLOCK:]
    for offset in SIDES:
        start(functools.partial(send_drive, 1), offset)
    ones = jnp.ones((8, frames_here), bf16)

    def level_of(rows):
        return (dot(ones, rows, NT) * (1.0 / frames_here)).astype(bf16)

    levels = []

    def foresee(rows):
        level = level_of(rows)
        for d in range(1, shares):
            beyond = pl.ds(first_of(partner(d), whole_rows), part_rows)
            guess[len(levels), d - 1] = dot(level, act[:, beyond])
        levels.append(level.astype(f32))

    foresee(spread[0])

    for offset in SIDES:
        arrive(send_diag, offset)
    line = lax.broadcasted_iota(jnp.int32, (BLOCK, three), 0)
    column = lax.broadcasted_iota(jnp.int32, (BLOCK, three), 1)
    rates = []
    for turn in range(2):
        diagonal = own_diagonal[place(turn, 1) : place(turn, 1) + BLOCK]
        for offset in SIDES:
            theirs = jnp.where(column == line + place(turn, 1 - offset), diag_in[side(-offset), 0:1, :], 0.0)
            diagonal += jnp.sum(theirs, axis=1, keepdims=True)
        rates.append(1.0 / (diagonal + 1.0))

    before = [around[strip(turn, 1), :] for turn in range(2)]
    corr_late = halves(corr[half:, :half])
    for offset in SIDES:
        arrive(functools.partial(send_drive, 0), offset)
    wanted = drive[strip(0, 1), :] + side_drive[0, 0] + side_drive[1, 0]
    after_first = jnp.maximum(before[0] + wanted * rates[0], 0.0)
    near_first, rest_first = halves(after_first)
    near[strip(0, 1), :] = near_first
    for offset in SIDES:
        start(functools.partial(send_near, 0), offset)
    rest_out[...] = rest_first
    for offset in SIDES:
        start(send_rest, offset)
    for d in range(1, shares):
        send_far(0, d).start()

    def total(rows):
        return jnp.sum(rows.astype(f32), axis=1, keepdims=True)

    def parts(band, only=None):
        at, size = bands[band]
        known = near[at : at + size, :]
        weight = total(known)
        for c in range(len(spans[band])) if only is None else only:
            begin, length = spans[band][c]
            for d in range(1, shares):
                rows = pl.ds(first_of(partner(d), whole_rows + begin), length)
                part = dot(known, frames_ref[rows, :], NT) - weight * guess[min(band, 2), d - 1, 0:1, begin : begin + length]
                part_out[d - 1, at : at + size, begin : begin + length] = part.astype(bf16)
                send_part(d, band, c).start()

    parts(0)
    foresee(jnp.concatenate([near_first, spread[0][BLOCK:]], axis=0))

    for offset in SIDES:
        arrive(functools.partial(send_near, 0), offset)
    parts(1, (0,))
    for offset in SIDES:
        arrive(send_rest, offset)
    change = [after_first - before[0]]
    for window in (0, 2):
        there = near[strip(0, window), :].astype(f32) + rest_in[window // 2].astype(f32)
        change.append(there - around[strip(0, window), :])
    change = halves(jnp.concatenate(change, axis=0))
    extra[BLOCK:, :] = -product([x[BLOCK:] for x in corr_late], change)
    for offset in SIDES:
        start(send_extra, offset)
    parts(1, range(1, len(spans[1])))
    extra[:BLOCK, :] = -product([x[:BLOCK] for x in corr_late], change)
    foresee(jnp.concatenate([near[:half, :], spread[0][half:]], axis=0))
    line = lax.broadcasted_iota(jnp.int32, (8, three), 0)
    hint_out[...] = jnp.where(line == 0, levels[0], jnp.where(line == 1, levels[1], levels[2]))
    for d in range(1, shares):
        send_hint(d).start()

    for d in range(1, shares):
        send_far(0, d).wait_recv()
        for offset in SIDES:
            start(functools.partial(relay, 0, d), offset)

    for offset in SIDES:
        arrive(functools.partial(send_drive, 1), offset)
        arrive(send_extra, offset)
    wanted = drive[strip(1, 1), :] + side_drive[0, 1] + side_drive[1, 1] + extra[0:BLOCK, :] + extra_in[0] + extra_in[1]
    after_second = jnp.maximum(before[1] + wanted * rates[1], 0.0)
    near[strip(1, 1), :] = after_second.astype(bf16)
    for offset in SIDES:
        start(functools.partial(send_near, 1), offset)
    for d in range(1, shares):
        send_far(1, d).start()
    parts(2)
    for block in range(2):
        updated_out[block * BLOCK : (block + 1) * BLOCK, :] = visit(block, 1, after_first, after_second)
    for offset in SIDES:
        arrive(functools.partial(send_near, 1), offset)
    parts(3)

    for d in range(1, shares):
        send_far(1, d).wait_recv()
        for offset in SIDES:
            start(functools.partial(relay, 1, d), offset)

    known = near[...]
    regions = [(begin, min(512, share_rows - begin)) for begin in range(whole_rows, share_rows, 512)]
    for begin, length in [(0, whole_rows)] + regions:
        mix[:, begin : begin + length] = dot(known, frames_ref[pl.ds(first_of(mine, begin), length), :], NT)

    for d in range(1, shares):
        for turn in range(2):
            for offset in SIDES:
                arrive(functools.partial(relay, turn, d), offset)
    gram = dot(known, known, NT)
    for d in range(1, shares):
        gram += dot(near_far[d - 1], near_far[d - 1], NT)
    line = lax.broadcasted_iota(jnp.int32, (three, three), 0)
    column = lax.broadcasted_iota(jnp.int32, (three, three), 1)
    scale = jnp.sum(jnp.where(line == column, gram, 0.0), axis=1, keepdims=True) + 1.0
    rate = 1.0 / scale
    grams = []
    for turn in range(2):
        high, low = halves(gram[turn * half : (turn + 1) * half])
        grams.append((jnp.concatenate([high, low], axis=0), high[:, :half]))

    def step_one(begin, length):
        here, cols = pl.ds(first_of(mine, begin), length), slice(begin, begin + length)
        active = act[:, here]
        fitted = dot(grams[0][0], active)
        left_over = mix[:half, cols] - fitted[:half] - fitted[half:]
        grown = active[:half].astype(f32) + left_over * rate[:half]
        after = jnp.maximum(grown, 0.0) * keep[:half, here].astype(f32)
        high, low = halves(after)
        shaped[:, cols] = high
        fitted = dot(grams[1][0], jnp.concatenate([high, active[half:]], axis=0))
        mix[half:, cols] += active[half:].astype(f32) * scale[half:] - fitted[:half] - fitted[half:] - dot(grams[1][1], low)

    def step_two(begin, length):
        here, cols = pl.ds(first_of(mine, begin), length), slice(begin, begin + length)
        after = jnp.maximum(mix[half:, cols] * rate[half:], 0.0) * keep[half:, here].astype(f32)
        second = after.astype(bf16)
        for window in range(3):
            row = place(0, window)
            for block in range(2):
                out = window * width + block * BLOCK
                refined_out[out : out + BLOCK, cols] = visit(
                    block, window, shaped[row : row + BLOCK, cols], second[row : row + BLOCK])

    for d in range(1, shares):
        for p in range(whole_pieces):
            send_frames(d, p).wait_recv()
        mix[:, :whole_rows] += dot(near_far[d - 1], frames_in[d - 1], NT)
    step_one(0, whole_rows)
    step_two(0, whole_rows)

    for d in range(1, shares):
        send_hint(d).wait_recv()
    weights = [total(near_far[d - 1]) for d in range(1, shares)]
    for d in range(1, shares):
        for band in range(2):
            for c in range(len(spans[band])):
                send_part(d, band, c).wait_recv()
    for begin, length in regions:
        here, cols = pl.ds(first_of(mine, begin), length), slice(begin, begin + length)
        for d in range(1, shares):
            guesses = dot(hint_in[d - 1].astype(bf16), act[:, here])
            near_part = part_in[d - 1, :half, begin - whole_rows : begin - whole_rows + length].astype(f32)
            weight = weights[d - 1]
            mix[:BLOCK, cols] += near_part[:BLOCK] + weight[:BLOCK] * guesses[0:1]
            mix[BLOCK:half, cols] += near_part[BLOCK:] + weight[BLOCK:half] * guesses[1:2]
            mix[half:, cols] += weight[half:] * guesses[2:3]
        step_one(begin, length)
    for offset in SIDES:
        for copy in (send_traces, send_diag, send_rest, send_extra):
            left(copy, offset)
        for turn in range(2):
            left(functools.partial(send_drive, turn), offset)
            left(functools.partial(send_near, turn), offset)
            for d in range(1, shares):
                left(functools.partial(relay, turn, d), offset)
    for d in range(1, shares):
        send_hint(d).wait_send()
        for turn in range(2):
            send_far(turn, d).wait_send()
        for p in range(whole_pieces):
            send_frames(d, p).wait_send()
        for band in range(2):
            for c in range(len(spans[band])):
                send_part(d, band, c).wait_send()
    for d in range(1, shares):
        send_part(d, 2, 0).wait_recv()
    for c, (begin, length) in enumerate(spans[3]):
        cols = slice(whole_rows + begin, whole_rows + begin + length)
        for d in range(1, shares):
            send_part(d, 3, c).wait_recv()
            mix[half:, cols] += part_in[d - 1, half:, begin : begin + length].astype(f32)
        step_two(whole_rows + begin, length)
    for d in range(1, shares):
        for band in (2, 3):
            for c in range(len(spans[band])):
                send_part(d, band, c).wait_send()


def deliver_kernel(refined_ref, updated_ref, refined_out, updated_out, sem):
    rows = refined_ref.shape[0] // 4
    moves = [(updated_ref, updated_out)]
    for i in range(4):
        part = pl.ds(i * rows, rows)
        moves.append((refined_ref.at[part], refined_out.at[part]))
    copies = [pltpu.make_async_copy(a, b, sem.at[i]) for i, (a, b) in enumerate(moves)]
    for copy in copies:
        copy.start()
    for copy in copies:
        copy.wait()


def deliver(refined, updated):
    refined, updated = (pltpu.with_memory_space_constraint(x, pltpu.VMEM) for x in (refined, updated))
    like = [jax.ShapeDtypeStruct(x.shape, x.dtype) for x in (refined, updated)]
    anywhere = pl.BlockSpec(memory_space=pl.ANY)
    refined, updated = pl.pallas_call(
        deliver_kernel, out_shape=like, in_specs=[anywhere] * 2, out_specs=[anywhere] * 2,
        scratch_shapes=[pltpu.SemaphoreType.DMA((5,))],
    )(refined, updated)
    return refined.T, updated


def cut(rows):
    early, late = (512, 256) if rows > 512 else (128, 128)
    front = [early, rows - early] if rows > early else [rows]
    back = [rows - late, late] if rows > late else [rows]
    return [front, front, [rows], back]


def shards(owners, shares, frames, footprints, support, traces, block_order):
    pixels, frames_here = frames.shape
    width = traces.shape[0]
    three = 3 * width
    share_rows = pixels // shares
    whole_rows = max(share_rows * WHOLE // 16 // 128, 1) * 128
    part_rows = share_rows - whole_rows
    chunks = cut(part_rows)
    others = shares - 1
    groups = 2
    vmem, dma = pltpu.VMEM, pltpu.SemaphoreType.DMA
    refined, updated = pl.pallas_call(
        functools.partial(kernel, owners, shares, chunks),
        out_shape=(pltpu.VMEM((three, share_rows), bf16), pltpu.VMEM(traces.shape, f32)),
        in_specs=[pl.BlockSpec(memory_space=pltpu.HBM)] * 5,
        out_specs=[pl.BlockSpec(memory_space=pltpu.VMEM)] * 2,
        scratch_shapes=[
            pltpu.SMEM(block_order.shape[::-1], jnp.int32),
            vmem(frames.shape, bf16),
            vmem((three, pixels), bf16),
            vmem(support.shape[::-1], jnp.int32),
            vmem((3,) + traces.shape, f32),
            vmem((three, pixels), bf16),
            vmem((three, pixels), bf16),
            vmem((three, frames_here), f32),
            vmem((three, frames_here), f32),
            vmem((three, three), f32),
            vmem((8, three), f32),
            vmem((2, 8, three), f32),
            vmem((2, 2, BLOCK, frames_here), f32),
            vmem((BLOCK, frames_here), bf16),
            vmem((2, BLOCK, frames_here), bf16),
            vmem((3 * BLOCK, frames_here), f32),
            vmem((2, BLOCK, frames_here), f32),
            vmem((three, frames_here), bf16),
            vmem((others, three, frames_here), bf16),
            vmem((3, others, 8, part_rows), f32),
            vmem((8, three), f32),
            vmem((others, 8, three), f32),
            vmem((others, whole_rows, frames_here), bf16),
            vmem((others, three, part_rows), bf16),
            vmem((others, three, part_rows), bf16),
            vmem((three, share_rows), f32),
            vmem((three // 2, share_rows), bf16),
            dma((groups + 2, 2)),
            dma((2,)), dma((2,)), dma((2,)), dma((2,)), dma((2, 2)), dma((2, 2)),
            dma((2,)), dma((2,)), dma((2,)), dma((2,)), dma((2, 2)), dma((2, 2)),
            dma((others, 2)), dma((others, 2)), dma((others, 2, 2)), dma((others, 2, 2)),
            dma((others,)), dma((others,)),
            dma((others, 1)), dma((others, 1)),
            dma((others, 4, 2)), dma((others, 4, 2)),
        ],
        compiler_params=pltpu.CompilerParams(
            collective_id=0, has_side_effects=True, vmem_limit_bytes=56 * 1024 * 1024
        ),
    )(block_order.T, frames, footprints.T, support.T, traces)
    return deliver(refined, updated)


def solution(mesh):
    in_specs = (P("pix", "frm"), P("pix", None), P("pix", None), P("pix", "frm"), P())
    out_specs = (P(("pix", "frm"), None), P("pix", "frm"))
    body = functools.partial(shards, mesh.shape["pix"], mesh.shape["frm"])
    return jax.shard_map(body, mesh=mesh, in_specs=in_specs, out_specs=out_specs, check_vma=False)
```

```python
import functools

import jax
import jax.numpy as jnp
from jax import lax
from jax.experimental import pallas as pl
from jax.experimental.pallas import tpu as pltpu
from jax.sharding import PartitionSpec as P

BLOCK = 32
TILE = 16
MESH = pl.DeviceIdType.MESH
SIDES = (-1, 1)
WINDOWS = (1, 0, 2)
WHOLE = 3
f32, bf16 = jnp.float32, jnp.bfloat16
NT = ((1,), (1,))


def dot(a, b, dims=((1,), (0,))):
    return lax.dot_general(a, b, (dims, ((), ())), preferred_element_type=f32)


def halves(x):
    high = x.astype(bf16)
    return high, (x - high.astype(f32)).astype(bf16)


def place(turn, window):
    return (turn * 3 + WINDOWS.index(window)) * BLOCK


def strip(turn, window):
    return pl.ds(place(turn, window), BLOCK)


def product(a, b):
    (a_high, a_low), (high, low) = a, b
    both = dot(jnp.concatenate([a_high, a_low], axis=0), high)
    n = a_high.shape[0]
    return both[:n] + both[n:] + dot(a_high, low)


def kernel(
    owners, shares, chunks, order_hbm, frames_hbm, foot_hbm, support_hbm, traces_hbm, refined_out, updated_out,
    order_ref, frames_ref, foot_ref, support_ref, traces_ref, traces_near, late_out, late_in, act, keep, around, drive, corr, diag_out, diag_in, side_drive,
    rest_out, rest_in, extra, extra_in, near, near_far, guess, hint_out, hint_in, frames_in, part_out, part_in, mix, shaped,
    in_sem, a_send, a_recv, b_send, b_recv, c_send, c_recv, d_send, d_recv, e_send, e_recv, g_send, g_recv,
    h_send, h_recv, i_send, i_recv, j_send, j_recv, k_send, k_recv, l_send, l_recv, m_send, m_recv,
):
    slab, mine = lax.axis_index("pix"), lax.axis_index("frm")
    pixels, frames_here = frames_ref.shape
    three = act.shape[0]
    half = three // 2
    width = three // 3
    share_rows = pixels // shares
    whole_rows = frames_in.shape[1]
    part_rows = share_rows - whole_rows
    whole_pieces = k_send.shape[1]
    piece = whole_rows // whole_pieces
    spans = [[(sum(sizes[:i]), size) for i, size in enumerate(sizes)] for sizes in chunks]
    barrier = pltpu.get_barrier_semaphore()

    def present(offset):
        return slab > 0 if offset < 0 else slab < owners - 1

    def partner(d):
        return lax.rem(mine + d, shares)

    for offset in SIDES:
        @pl.when(present(offset))
        def _():
            pl.semaphore_signal(barrier, inc=1, device_id=(slab + offset, mine), device_id_type=MESH)
    for d in range(1, shares):
        pl.semaphore_signal(barrier, inc=1, device_id=(slab, partner(d)), device_id_type=MESH)

    groups = in_sem.shape[0] - 2
    chunk = pixels // groups

    def bring(c):
        rows = pl.ds(c * chunk, chunk)
        return [pltpu.make_async_copy(foot_hbm.at[:, rows], foot_ref.at[:, rows], in_sem.at[c, 0]),
                pltpu.make_async_copy(frames_hbm.at[rows], frames_ref.at[rows], in_sem.at[c, 1])]

    fetch_support = pltpu.make_async_copy(support_hbm, support_ref, in_sem.at[groups, 0])
    fetch_traces = pltpu.make_async_copy(traces_hbm, traces_ref, in_sem.at[groups, 1])
    fetch_order = pltpu.make_async_copy(order_hbm, order_ref, in_sem.at[groups + 1, 0])
    fetch_traces.start()
    fetch_support.start()
    fetch_order.start()
    for c in range(groups):
        for copy in bring(c):
            copy.start()

    def side(offset):
        return 1 if offset < 0 else 0

    for offset in SIDES:
        @pl.when(jnp.logical_not(present(offset)))
        def _():
            here = side(-offset)
            diag_in[here] = jnp.zeros(diag_in.shape[1:], f32)
            side_drive[here] = jnp.zeros(side_drive.shape[1:], f32)
            rest_in[here] = jnp.zeros(rest_in.shape[1:], bf16)
            extra_in[here] = jnp.zeros(extra_in.shape[1:], f32)
            late_in[here] = jnp.zeros(late_in.shape[1:], bf16)
            for part in range(2):
                traces_near[part, 1 + offset] = jnp.zeros(traces_near.shape[2:], bf16)
            for turn in range(2):
                near[strip(turn, 1 + offset), :] = jnp.zeros((BLOCK, frames_here), bf16)
                for d in range(1, shares):
                    near_far[d - 1, strip(turn, 1 + offset), :] = jnp.zeros((BLOCK, frames_here), bf16)

    def remote(src, dst, send, recv, to):
        return pltpu.make_async_remote_copy(
            src_ref=src, dst_ref=dst, send_sem=send, recv_sem=recv, device_id=to, device_id_type=MESH)

    def beside(offset):
        return slab + offset, mine

    def send_traces(part, offset):
        s = side(offset)
        return remote(traces_near.at[part, 1], traces_near.at[part, 1 - offset], a_send.at[s, part], a_recv.at[s, part],
                      beside(offset))

    def send_late(offset):
        s = side(offset)
        return remote(late_out.at[pl.ds(place(0, 1 + offset) - BLOCK, BLOCK)], late_in.at[s], m_send.at[s], m_recv.at[s],
                      beside(offset))

    def send_diag(offset):
        s = side(offset)
        return remote(diag_out, diag_in.at[s], b_send.at[s], b_recv.at[s], beside(offset))

    def send_drive(turn, offset):
        s = side(offset)
        return remote(drive.at[strip(turn, 1 + offset)], side_drive.at[s, turn], c_send.at[s, turn], c_recv.at[s, turn],
                      beside(offset))

    def send_rest(offset):
        s = side(offset)
        return remote(rest_out, rest_in.at[s], d_send.at[s], d_recv.at[s], beside(offset))

    def send_extra(offset):
        s = side(offset)
        return remote(extra.at[pl.ds(place(0, 1 + offset), BLOCK)], extra_in.at[s], e_send.at[s], e_recv.at[s], beside(offset))

    def send_near(turn, offset):
        s = side(offset)
        return remote(near.at[strip(turn, 1)], near.at[strip(turn, 1 - offset)], g_send.at[s, turn], g_recv.at[s, turn],
                      beside(offset))

    def send_far(turn, d):
        return remote(near.at[strip(turn, 1)], near_far.at[d - 1, strip(turn, 1)], h_send.at[d - 1, turn], h_recv.at[d - 1, turn],
                      (slab, partner(d)))

    def relay(turn, d, offset):
        s = side(offset)
        return remote(near_far.at[d - 1, strip(turn, 1)], near_far.at[d - 1, strip(turn, 1 - offset)],
                      i_send.at[d - 1, s, turn], i_recv.at[d - 1, s, turn], beside(offset))

    def send_hint(d):
        return remote(hint_out, hint_in.at[d - 1], j_send.at[d - 1], j_recv.at[d - 1], (slab, partner(d)))

    def first_of(who, row):
        return pl.multiple_of(who * share_rows + row, 128)

    def send_frames(d, p):
        return remote(frames_hbm.at[pl.ds(first_of(partner(d), p * piece), piece)], frames_in.at[d - 1, pl.ds(p * piece, piece)],
                      k_send.at[d - 1, p], k_recv.at[d - 1, p], (slab, partner(d)))

    mate = 1 - 2 * lax.rem(slab, 2)
    mate_row = pl.multiple_of((1 + (mate + 1) // 2) * BLOCK, BLOCK)
    other_row = pl.multiple_of((2 - (mate + 1) // 2) * BLOCK, BLOCK)
    bands = [pl.ds(turn * half + row, BLOCK) for turn in range(2) for row in (0, mate_row, other_row)]

    def send_part(d, band, c):
        where = (d - 1, bands[band], pl.ds(*spans[band][c]))
        return remote(part_out.at[where], part_in.at[where], l_send.at[d - 1, band, c], l_recv.at[d - 1, band, c], (slab, partner(d)))

    def start(copy, offset):
        @pl.when(present(offset))
        def _():
            copy(offset).start()

    def arrive(copy, offset):
        @pl.when(present(-offset))
        def _():
            copy(offset).wait_recv()

    def arrive_mate(copy):
        for offset in SIDES:
            @pl.when(jnp.logical_and(present(-offset), mate == -offset))
            def _():
                copy(offset).wait_recv()

    def arrive_other(copy):
        for offset in SIDES:
            @pl.when(jnp.logical_and(present(-offset), mate == offset))
            def _():
                copy(offset).wait_recv()

    def left(copy, offset):
        @pl.when(present(offset))
        def _():
            copy(offset).wait_send()

    def visited(turn, window):
        return order_ref[turn, jnp.clip(slab - 1 + window, 0, owners - 1)]

    def visit(turn, window, low, high):
        in_order = visited(0, window) == 0
        return jnp.where(in_order, low, high) if turn == 0 else jnp.where(in_order, high, low)

    def visit_all(load):
        pairs = {w: (load(w * width), load(w * width + BLOCK)) for w in WINDOWS}
        return [visit(turn, w, *pairs[w]) for turn in range(2) for w in WINDOWS]

    peers = present(-1).astype(jnp.int32) + present(1).astype(jnp.int32) + shares - 1
    pl.semaphore_wait(barrier, peers)
    for p in range(whole_pieces):
        for d in range(1, shares):
            send_frames(d, p).start()
    fetch_traces.wait()
    for part, value in enumerate(halves(traces_ref[...])):
        traces_near[part, 1] = value
        for offset in SIDES:
            start(functools.partial(send_traces, part), offset)

    usable = {0: (slab > 0).astype(f32), 1: 1.0, 2: (slab < owners - 1).astype(f32)}
    fetch_order.wait()
    fetch_support.wait()
    supported = jnp.concatenate(visit_all(
        lambda row: support_ref[row : row + BLOCK, :].astype(f32) * usable[row // width]), axis=0).astype(bf16)
    tiles = support_ref.shape[1]
    stretch = pixels // 4
    tile_of = lax.broadcasted_iota(jnp.int32, (tiles, stretch), 1) // TILE
    tile_is = lax.broadcasted_iota(jnp.int32, (tiles, stretch), 0)
    for c in range(4):
        spread = (tile_is == tile_of + c * (stretch // TILE)).astype(f32).astype(bf16)
        keep[:, c * stretch : (c + 1) * stretch] = dot(supported, spread).astype(bf16)

    for c in range(groups):
        rows = slice(c * chunk, (c + 1) * chunk)
        for copy in bring(c):
            copy.wait()
        active = jnp.concatenate(visit_all(lambda row: foot_ref[row : row + BLOCK, rows]), axis=0) * keep[:, rows]
        act[:, rows] = active
        together = dot(active, active, NT)
        corr[...] = together if c == 0 else corr[...] + together
        loads = dot(active, frames_ref[rows, :])
        drive[...] = loads if c == 0 else drive[...] + loads

    line = lax.broadcasted_iota(jnp.int32, (three, three), 0)
    column = lax.broadcasted_iota(jnp.int32, (three, three), 1)
    on_diagonal = jnp.where(line == column, corr[...], 0.0)
    diag_out[...] = jnp.broadcast_to(jnp.sum(on_diagonal, axis=0, keepdims=True), diag_out.shape)
    own_diagonal = jnp.sum(on_diagonal, axis=1, keepdims=True)
    for offset in SIDES:
        start(send_diag, offset)

    sides, rest = slice(BLOCK, half), [slice(0, BLOCK), slice(half, three)]
    corr_sides = halves(corr[sides, :])
    corr_rest = halves(jnp.concatenate([corr[r, :] for r in rest], axis=0))
    def ordered(part, windows):
        blank = jnp.zeros((BLOCK, frames_here), bf16)
        return [visit(turn, w, traces_near[part, w, :BLOCK, :], traces_near[part, w, BLOCK:, :]) if w in windows else blank
                for turn in range(2) for w in WINDOWS]

    own_low = jnp.concatenate(ordered(1, (1,)), axis=0)
    for offset in SIDES:
        arrive(functools.partial(send_traces, 0), offset)
    high = jnp.concatenate(ordered(0, WINDOWS), axis=0)
    drive[sides, :] -= product(corr_sides, (high, own_low))
    for offset in SIDES:
        start(functools.partial(send_drive, 0), offset)
    for turn in range(2):
        around[strip(turn, 1), :] = visit(turn, 1, traces_ref[:BLOCK, :], traces_ref[BLOCK:, :])
    for offset in SIDES:
        arrive(functools.partial(send_traces, 1), offset)
    low = jnp.concatenate(ordered(1, (0, 2)), axis=0)
    late_out[...] = (-dot(corr_sides[0], low)).astype(bf16)
    for offset in SIDES:
        start(send_late, offset)
    for turn in range(2):
        for window in (0, 2):
            row = place(turn, window)
            around[strip(turn, window), :] = high[row : row + BLOCK].astype(f32) + low[row : row + BLOCK].astype(f32)
    fitted = product(corr_rest, (high, own_low + low))
    drive[rest[0], :] -= fitted[:BLOCK]
    drive[rest[1], :] -= fitted[BLOCK:]
    ones = jnp.ones((8, frames_here), bf16)

    def level_of(rows):
        return (dot(ones, rows, NT) * (1.0 / frames_here)).astype(bf16)

    levels = []

    def foresee(rows):
        level = level_of(rows)
        for d in range(1, shares):
            beyond = pl.ds(first_of(partner(d), whole_rows), part_rows)
            guess[len(levels), d - 1] = dot(level, act[:, beyond])
        levels.append(level.astype(f32))

    foresee(high)

    for offset in SIDES:
        arrive(send_diag, offset)
    line = lax.broadcasted_iota(jnp.int32, (BLOCK, three), 0)
    column = lax.broadcasted_iota(jnp.int32, (BLOCK, three), 1)
    rates = []
    for turn in range(2):
        diagonal = own_diagonal[place(turn, 1) : place(turn, 1) + BLOCK]
        for offset in SIDES:
            theirs = jnp.where(column == line + place(turn, 1 - offset), diag_in[side(-offset), 0:1, :], 0.0)
            diagonal += jnp.sum(theirs, axis=1, keepdims=True)
        rates.append(1.0 / (diagonal + 1.0))

    before = [around[strip(turn, 1), :] for turn in range(2)]
    corr_late = halves(corr[half:, :half])
    for offset in SIDES:
        arrive(functools.partial(send_drive, 0), offset)
    wanted = drive[strip(0, 1), :] + side_drive[0, 0] + side_drive[1, 0]
    for offset in SIDES:
        arrive(send_late, offset)
    wanted += late_in[0].astype(f32) + late_in[1].astype(f32)
    after_first = jnp.maximum(before[0] + wanted * rates[0], 0.0)
    near_first, rest_first = halves(after_first)
    near[strip(0, 1), :] = near_first
    for offset in SIDES:
        start(functools.partial(send_near, 0), offset)
    for d in range(1, shares):
        send_far(0, d).start()

    def total(rows):
        return jnp.sum(rows.astype(f32), axis=1, keepdims=True)

    def parts(band):
        known = near[bands[band], :]
        weight = total(known)
        for c, (begin, length) in enumerate(spans[band]):
            for d in range(1, shares):
                rows = pl.ds(first_of(partner(d), whole_rows + begin), length)
                part = dot(known, frames_ref[rows, :], NT) - weight * guess[(0, 1, 1, 2, 2, 2)[band], d - 1, 0:1, begin : begin + length]
                part_out[d - 1, bands[band], begin : begin + length] = part.astype(bf16)
                send_part(d, band, c).start()

    parts(0)
    rest_out[...] = rest_first
    for offset in SIDES:
        start(send_rest, offset)
    for offset in SIDES:
        start(functools.partial(send_drive, 1), offset)
    foresee(jnp.concatenate([near_first, high[BLOCK:]], axis=0))

    arrive_mate(functools.partial(send_near, 0))
    parts(1)
    arrive_other(functools.partial(send_near, 0))
    for offset in SIDES:
        arrive(send_rest, offset)
    change = [after_first - before[0]]
    for window in (0, 2):
        there = near[strip(0, window), :].astype(f32) + rest_in[window // 2].astype(f32)
        change.append(there - around[strip(0, window), :])
    change = halves(jnp.concatenate(change, axis=0))
    extra[BLOCK:, :] = -product([x[BLOCK:] for x in corr_late], change)
    for offset in SIDES:
        start(send_extra, offset)
    parts(2)
    extra[:BLOCK, :] = -product([x[:BLOCK] for x in corr_late], change)
    foresee(jnp.concatenate([near[:half, :], high[half:]], axis=0))
    line = lax.broadcasted_iota(jnp.int32, (8, three), 0)
    hint_out[...] = jnp.where(line == 0, levels[0], jnp.where(line == 1, levels[1], levels[2]))
    for d in range(1, shares):
        send_hint(d).start()

    for d in range(1, shares):
        send_far(0, d).wait_recv()
        for offset in SIDES:
            start(functools.partial(relay, 0, d), offset)

    for offset in SIDES:
        arrive(functools.partial(send_drive, 1), offset)
        arrive(send_extra, offset)
    wanted = drive[strip(1, 1), :] + side_drive[0, 1] + side_drive[1, 1] + extra[0:BLOCK, :] + extra_in[0] + extra_in[1]
    after_second = jnp.maximum(before[1] + wanted * rates[1], 0.0)
    near[strip(1, 1), :] = after_second.astype(bf16)
    for offset in SIDES:
        start(functools.partial(send_near, 1), offset)
    for d in range(1, shares):
        send_far(1, d).start()
    parts(3)
    for block in range(2):
        updated_out[block * BLOCK : (block + 1) * BLOCK, :] = visit(block, 1, after_first, after_second)
    arrive_mate(functools.partial(send_near, 1))
    parts(4)
    arrive_other(functools.partial(send_near, 1))
    parts(5)

    for d in range(1, shares):
        send_far(1, d).wait_recv()
        for offset in SIDES:
            start(functools.partial(relay, 1, d), offset)

    known = near[...]
    regions = [(begin, min(512, share_rows - begin)) for begin in range(whole_rows, share_rows, 512)]
    for begin, length in [(0, whole_rows)] + regions:
        mix[:, begin : begin + length] = dot(known, frames_ref[pl.ds(first_of(mine, begin), length), :], NT)

    for d in range(1, shares):
        for turn in range(2):
            for offset in SIDES:
                arrive(functools.partial(relay, turn, d), offset)
    gram = dot(known, known, NT)
    for d in range(1, shares):
        gram += dot(near_far[d - 1], near_far[d - 1], NT)
    line = lax.broadcasted_iota(jnp.int32, (three, three), 0)
    column = lax.broadcasted_iota(jnp.int32, (three, three), 1)
    scale = jnp.sum(jnp.where(line == column, gram, 0.0), axis=1, keepdims=True) + 1.0
    rate = 1.0 / scale
    grams = []
    for turn in range(2):
        high, low = halves(gram[turn * half : (turn + 1) * half])
        grams.append((jnp.concatenate([high, low], axis=0), high[:, :half]))

    def step_one(begin, length):
        here, cols = pl.ds(first_of(mine, begin), length), slice(begin, begin + length)
        active = act[:, here]
        fitted = dot(grams[0][0], active)
        left_over = mix[:half, cols] - fitted[:half] - fitted[half:]
        grown = active[:half].astype(f32) + left_over * rate[:half]
        after = jnp.maximum(grown, 0.0) * keep[:half, here].astype(f32)
        high, low = halves(after)
        shaped[:, cols] = high
        fitted = dot(grams[1][0], jnp.concatenate([high, active[half:]], axis=0))
        mix[half:, cols] += active[half:].astype(f32) * scale[half:] - fitted[:half] - fitted[half:] - dot(grams[1][1], low)

    def step_two(begin, length):
        here, cols = pl.ds(first_of(mine, begin), length), slice(begin, begin + length)
        after = jnp.maximum(mix[half:, cols] * rate[half:], 0.0) * keep[half:, here].astype(f32)
        second = after.astype(bf16)
        for window in range(3):
            row = place(0, window)
            for block in range(2):
                out = window * width + block * BLOCK
                refined_out[out : out + BLOCK, cols] = visit(
                    block, window, shaped[row : row + BLOCK, cols], second[row : row + BLOCK])

    for d in range(1, shares):
        for p in range(whole_pieces):
            send_frames(d, p).wait_recv()
        mix[:, :whole_rows] += dot(near_far[d - 1], frames_in[d - 1], NT)
    step_one(0, whole_rows)
    step_two(0, whole_rows)

    for d in range(1, shares):
        send_hint(d).wait_recv()
    weights = [total(near_far[d - 1]) for d in range(1, shares)]
    for d in range(1, shares):
        for band in range(3):
            for c in range(len(spans[band])):
                send_part(d, band, c).wait_recv()
    for begin, length in regions:
        here, cols = pl.ds(first_of(mine, begin), length), slice(begin, begin + length)
        for d in range(1, shares):
            guesses = dot(hint_in[d - 1].astype(bf16), act[:, here])
            near_part = part_in[d - 1, :half, begin - whole_rows : begin - whole_rows + length].astype(f32)
            weight = weights[d - 1]
            mix[:BLOCK, cols] += near_part[:BLOCK] + weight[:BLOCK] * guesses[0:1]
            mix[BLOCK:half, cols] += near_part[BLOCK:] + weight[BLOCK:half] * guesses[1:2]
            mix[half:, cols] += weight[half:] * guesses[2:3]
        step_one(begin, length)
    for offset in SIDES:
        for copy in (send_late, send_diag, send_rest, send_extra):
            left(copy, offset)
        for turn in range(2):
            left(functools.partial(send_traces, turn), offset)
            left(functools.partial(send_drive, turn), offset)
            left(functools.partial(send_near, turn), offset)
            for d in range(1, shares):
                left(functools.partial(relay, turn, d), offset)
    for d in range(1, shares):
        send_hint(d).wait_send()
        for turn in range(2):
            send_far(turn, d).wait_send()
        for p in range(whole_pieces):
            send_frames(d, p).wait_send()
        for band in range(3):
            for c in range(len(spans[band])):
                send_part(d, band, c).wait_send()
    for d in range(1, shares):
        send_part(d, 3, 0).wait_recv()
        send_part(d, 4, 0).wait_recv()
    for c, (begin, length) in enumerate(spans[5]):
        cols = slice(whole_rows + begin, whole_rows + begin + length)
        for d in range(1, shares):
            send_part(d, 5, c).wait_recv()
            mix[half:, cols] += part_in[d - 1, half:, begin : begin + length].astype(f32)
        step_two(whole_rows + begin, length)
    for d in range(1, shares):
        for band in range(3, 6):
            for c in range(len(spans[band])):
                send_part(d, band, c).wait_send()


def deliver_kernel(refined_ref, updated_ref, refined_out, updated_out, sem):
    rows = refined_ref.shape[0] // 4
    moves = [(updated_ref, updated_out)]
    for i in range(4):
        part = pl.ds(i * rows, rows)
        moves.append((refined_ref.at[part], refined_out.at[part]))
    copies = [pltpu.make_async_copy(a, b, sem.at[i]) for i, (a, b) in enumerate(moves)]
    for copy in copies:
        copy.start()
    for copy in copies:
        copy.wait()


def deliver(refined, updated):
    refined, updated = (pltpu.with_memory_space_constraint(x, pltpu.VMEM) for x in (refined, updated))
    like = [jax.ShapeDtypeStruct(x.shape, x.dtype) for x in (refined, updated)]
    anywhere = pl.BlockSpec(memory_space=pl.ANY)
    refined, updated = pl.pallas_call(
        deliver_kernel, out_shape=like, in_specs=[anywhere] * 2, out_specs=[anywhere] * 2,
        scratch_shapes=[pltpu.SemaphoreType.DMA((5,))],
    )(refined, updated)
    return refined.T, updated


def cut(rows):
    early, late = (512, 256) if rows > 512 else (128, 128)
    front = [early, rows - early] if rows > early else [rows]
    back = [rows - late, late] if rows > late else [rows]
    return [front, [rows], [rows], [rows], [rows], back]


def shards(owners, shares, frames, footprints, support, traces, block_order):
    pixels, frames_here = frames.shape
    width = traces.shape[0]
    three = 3 * width
    share_rows = pixels // shares
    whole_rows = max(share_rows * WHOLE // 16 // 128, 1) * 128
    part_rows = share_rows - whole_rows
    chunks = cut(part_rows)
    others = shares - 1
    groups = 2
    vmem, dma = pltpu.VMEM, pltpu.SemaphoreType.DMA
    refined, updated = pl.pallas_call(
        functools.partial(kernel, owners, shares, chunks),
        out_shape=(pltpu.VMEM((three, share_rows), bf16), pltpu.VMEM(traces.shape, f32)),
        in_specs=[pl.BlockSpec(memory_space=pltpu.HBM)] * 5,
        out_specs=[pl.BlockSpec(memory_space=pltpu.VMEM)] * 2,
        scratch_shapes=[
            pltpu.SMEM(block_order.shape[::-1], jnp.int32),
            vmem(frames.shape, bf16),
            vmem((three, pixels), bf16),
            vmem(support.shape[::-1], jnp.int32),
            vmem(traces.shape, f32),
            vmem((2, 3) + traces.shape, bf16),
            vmem((2 * BLOCK, frames_here), bf16),
            vmem((2, BLOCK, frames_here), bf16),
            vmem((three, pixels), bf16),
            vmem((three, pixels), bf16),
            vmem((three, frames_here), f32),
            vmem((three, frames_here), f32),
            vmem((three, three), f32),
            vmem((8, three), f32),
            vmem((2, 8, three), f32),
            vmem((2, 2, BLOCK, frames_here), f32),
            vmem((BLOCK, frames_here), bf16),
            vmem((2, BLOCK, frames_here), bf16),
            vmem((3 * BLOCK, frames_here), f32),
            vmem((2, BLOCK, frames_here), f32),
            vmem((three, frames_here), bf16),
            vmem((others, three, frames_here), bf16),
            vmem((3, others, 8, part_rows), f32),
            vmem((8, three), f32),
            vmem((others, 8, three), f32),
            vmem((others, whole_rows, frames_here), bf16),
            vmem((others, three, part_rows), bf16),
            vmem((others, three, part_rows), bf16),
            vmem((three, share_rows), f32),
            vmem((three // 2, share_rows), bf16),
            dma((groups + 2, 2)),
            dma((2, 2)), dma((2, 2)), dma((2,)), dma((2,)), dma((2, 2)), dma((2, 2)),
            dma((2,)), dma((2,)), dma((2,)), dma((2,)), dma((2, 2)), dma((2, 2)),
            dma((others, 2)), dma((others, 2)), dma((others, 2, 2)), dma((others, 2, 2)),
            dma((others,)), dma((others,)),
            dma((others, 1)), dma((others, 1)),
            dma((others, 6, 2)), dma((others, 6, 2)), dma((2,)), dma((2,)),
        ],
        compiler_params=pltpu.CompilerParams(
            collective_id=0, has_side_effects=True, vmem_limit_bytes=56 * 1024 * 1024
        ),
    )(block_order.T, frames, footprints.T, support.T, traces)
    return deliver(refined, updated)


def solution(mesh):
    in_specs = (P("pix", "frm"), P("pix", None), P("pix", None), P("pix", "frm"), P())
    out_specs = (P(("pix", "frm"), None), P("pix", "frm"))
    body = functools.partial(shards, mesh.shape["pix"], mesh.shape["frm"])
    return jax.shard_map(body, mesh=mesh, in_specs=in_specs, out_specs=out_specs, check_vma=False)
```

```python
import functools

import jax
import jax.numpy as jnp
from jax import lax
from jax.experimental import pallas as pl
from jax.experimental.pallas import tpu as pltpu
from jax.sharding import PartitionSpec as P

BLOCK = 32
TILE = 16
MESH = pl.DeviceIdType.MESH
SIDES = (-1, 1)
WINDOWS = (1, 0, 2)
WHOLE = 3
f32, bf16 = jnp.float32, jnp.bfloat16
NT = ((1,), (1,))


def dot(a, b, dims=((1,), (0,))):
    return lax.dot_general(a, b, (dims, ((), ())), preferred_element_type=f32)


def halves(x):
    high = x.astype(bf16)
    return high, (x - high.astype(f32)).astype(bf16)


def place(turn, window):
    return (turn * 3 + WINDOWS.index(window)) * BLOCK


def strip(turn, window):
    return pl.ds(place(turn, window), BLOCK)


def product(a, b):
    (a_high, a_low), (high, low) = a, b
    both = dot(jnp.concatenate([a_high, a_low], axis=0), high)
    n = a_high.shape[0]
    return both[:n] + both[n:] + dot(a_high, low)


def kernel(
    owners, shares, chunks, order_hbm, frames_hbm, foot_hbm, support_hbm, traces_hbm, refined_out, updated_out,
    order_ref, frames_ref, foot_ref, support_ref, traces_ref, traces_near, late_out, late_in, drive_out, drive_in, act, keep, around, drive, corr, diag_out, diag_in, side_drive,
    rest_out, rest_in, extra, extra_in, near, near_far, guess, hint_out, hint_in, frames_in, part_out, part_in, mix, shaped,
    in_sem, a_send, a_recv, b_send, b_recv, c_send, c_recv, d_send, d_recv, e_send, e_recv, g_send, g_recv,
    h_send, h_recv, i_send, i_recv, j_send, j_recv, k_send, k_recv, l_send, l_recv, m_send, m_recv,
):
    slab, mine = lax.axis_index("pix"), lax.axis_index("frm")
    pixels, frames_here = frames_ref.shape
    three = act.shape[0]
    half = three // 2
    width = three // 3
    share_rows = pixels // shares
    whole_rows = frames_in.shape[1]
    part_rows = share_rows - whole_rows
    whole_pieces = k_send.shape[1]
    piece = whole_rows // whole_pieces
    spans = [[(sum(sizes[:i]), size) for i, size in enumerate(sizes)] for sizes in chunks]
    barrier = pltpu.get_barrier_semaphore()

    def present(offset):
        return slab > 0 if offset < 0 else slab < owners - 1

    def partner(d):
        return lax.rem(mine + d, shares)

    for offset in SIDES:
        @pl.when(present(offset))
        def _():
            pl.semaphore_signal(barrier, inc=1, device_id=(slab + offset, mine), device_id_type=MESH)
    for d in range(1, shares):
        pl.semaphore_signal(barrier, inc=1, device_id=(slab, partner(d)), device_id_type=MESH)

    groups = in_sem.shape[0] - 2
    chunk = pixels // groups

    def bring(c):
        rows = pl.ds(c * chunk, chunk)
        return [pltpu.make_async_copy(foot_hbm.at[:, rows], foot_ref.at[:, rows], in_sem.at[c, 0]),
                pltpu.make_async_copy(frames_hbm.at[rows], frames_ref.at[rows], in_sem.at[c, 1])]

    fetch_support = pltpu.make_async_copy(support_hbm, support_ref, in_sem.at[groups, 0])
    fetch_traces = pltpu.make_async_copy(traces_hbm, traces_ref, in_sem.at[groups, 1])
    fetch_order = pltpu.make_async_copy(order_hbm, order_ref, in_sem.at[groups + 1, 0])
    fetch_traces.start()
    fetch_support.start()
    fetch_order.start()
    for c in range(groups):
        for copy in bring(c):
            copy.start()

    def side(offset):
        return 1 if offset < 0 else 0

    for offset in SIDES:
        @pl.when(jnp.logical_not(present(offset)))
        def _():
            here = side(-offset)
            diag_in[here] = jnp.zeros(diag_in.shape[1:], f32)
            side_drive[here] = jnp.zeros(side_drive.shape[1:], f32)
            rest_in[here] = jnp.zeros(rest_in.shape[1:], bf16)
            extra_in[here] = jnp.zeros(extra_in.shape[1:], f32)
            drive_in[here] = jnp.zeros(drive_in.shape[1:], bf16)
            late_in[here] = jnp.zeros(late_in.shape[1:], bf16)
            for part in range(2):
                traces_near[part, 1 + offset] = jnp.zeros(traces_near.shape[2:], bf16)
            for turn in range(2):
                near[strip(turn, 1 + offset), :] = jnp.zeros((BLOCK, frames_here), bf16)
                for d in range(1, shares):
                    near_far[d - 1, strip(turn, 1 + offset), :] = jnp.zeros((BLOCK, frames_here), bf16)

    def remote(src, dst, send, recv, to):
        return pltpu.make_async_remote_copy(
            src_ref=src, dst_ref=dst, send_sem=send, recv_sem=recv, device_id=to, device_id_type=MESH)

    def beside(offset):
        return slab + offset, mine

    def send_traces(part, offset):
        s = side(offset)
        return remote(traces_near.at[part, 1], traces_near.at[part, 1 - offset], a_send.at[s, part], a_recv.at[s, part],
                      beside(offset))

    def send_late(offset):
        s = side(offset)
        return remote(late_out.at[pl.ds(place(0, 1 + offset) - BLOCK, BLOCK)], late_in.at[s], m_send.at[s], m_recv.at[s],
                      beside(offset))

    def send_diag(offset):
        s = side(offset)
        return remote(diag_out, diag_in.at[s], b_send.at[s], b_recv.at[s], beside(offset))

    def send_drive_high(offset):
        s = side(offset)
        return remote(drive_out.at[pl.ds(place(0, 1 + offset) - BLOCK, BLOCK)], drive_in.at[s], c_send.at[s, 0], c_recv.at[s, 0],
                      beside(offset))

    def send_drive(offset):
        s = side(offset)
        return remote(drive.at[strip(1, 1 + offset)], side_drive.at[s], c_send.at[s, 1], c_recv.at[s, 1], beside(offset))

    def send_rest(offset):
        s = side(offset)
        return remote(rest_out, rest_in.at[s], d_send.at[s], d_recv.at[s], beside(offset))

    def send_extra(offset):
        s = side(offset)
        return remote(extra.at[pl.ds(place(0, 1 + offset), BLOCK)], extra_in.at[s], e_send.at[s], e_recv.at[s], beside(offset))

    def send_near(turn, offset):
        s = side(offset)
        return remote(near.at[strip(turn, 1)], near.at[strip(turn, 1 - offset)], g_send.at[s, turn], g_recv.at[s, turn],
                      beside(offset))

    def send_far(turn, d):
        return remote(near.at[strip(turn, 1)], near_far.at[d - 1, strip(turn, 1)], h_send.at[d - 1, turn], h_recv.at[d - 1, turn],
                      (slab, partner(d)))

    def relay(turn, d, offset):
        s = side(offset)
        return remote(near_far.at[d - 1, strip(turn, 1)], near_far.at[d - 1, strip(turn, 1 - offset)],
                      i_send.at[d - 1, s, turn], i_recv.at[d - 1, s, turn], beside(offset))

    def send_hint(d):
        return remote(hint_out, hint_in.at[d - 1], j_send.at[d - 1], j_recv.at[d - 1], (slab, partner(d)))

    def first_of(who, row):
        return pl.multiple_of(who * share_rows + row, 128)

    def send_frames(d, p):
        return remote(frames_hbm.at[pl.ds(first_of(partner(d), p * piece), piece)], frames_in.at[d - 1, pl.ds(p * piece, piece)],
                      k_send.at[d - 1, p], k_recv.at[d - 1, p], (slab, partner(d)))

    mate = 1 - 2 * lax.rem(slab, 2)
    mate_row = pl.multiple_of((1 + (mate + 1) // 2) * BLOCK, BLOCK)
    other_row = pl.multiple_of((2 - (mate + 1) // 2) * BLOCK, BLOCK)
    bands = [pl.ds(turn * half + row, BLOCK) for turn in range(2) for row in (0, mate_row, other_row)]

    def send_part(d, band, c):
        where = (d - 1, bands[band], pl.ds(*spans[band][c]))
        return remote(part_out.at[where], part_in.at[where], l_send.at[d - 1, band, c], l_recv.at[d - 1, band, c], (slab, partner(d)))

    def start(copy, offset):
        @pl.when(present(offset))
        def _():
            copy(offset).start()

    def arrive(copy, offset):
        @pl.when(present(-offset))
        def _():
            copy(offset).wait_recv()

    def arrive_mate(copy):
        for offset in SIDES:
            @pl.when(jnp.logical_and(present(-offset), mate == -offset))
            def _():
                copy(offset).wait_recv()

    def arrive_other(copy):
        for offset in SIDES:
            @pl.when(jnp.logical_and(present(-offset), mate == offset))
            def _():
                copy(offset).wait_recv()

    def left(copy, offset):
        @pl.when(present(offset))
        def _():
            copy(offset).wait_send()

    def visited(turn, window):
        return order_ref[turn, jnp.clip(slab - 1 + window, 0, owners - 1)]

    def visit(turn, window, low, high):
        in_order = visited(0, window) == 0
        return jnp.where(in_order, low, high) if turn == 0 else jnp.where(in_order, high, low)

    def visit_all(load):
        pairs = {w: (load(w * width), load(w * width + BLOCK)) for w in WINDOWS}
        return [visit(turn, w, *pairs[w]) for turn in range(2) for w in WINDOWS]

    peers = present(-1).astype(jnp.int32) + present(1).astype(jnp.int32) + shares - 1
    pl.semaphore_wait(barrier, peers)
    for p in range(whole_pieces):
        for d in range(1, shares):
            send_frames(d, p).start()
    fetch_traces.wait()
    for part, value in enumerate(halves(traces_ref[...])):
        traces_near[part, 1] = value
        for offset in SIDES:
            start(functools.partial(send_traces, part), offset)

    usable = {0: (slab > 0).astype(f32), 1: 1.0, 2: (slab < owners - 1).astype(f32)}
    fetch_order.wait()
    fetch_support.wait()
    supported = jnp.concatenate(visit_all(
        lambda row: support_ref[row : row + BLOCK, :].astype(f32) * usable[row // width]), axis=0).astype(bf16)
    tiles = support_ref.shape[1]
    stretch = pixels // 4
    tile_of = lax.broadcasted_iota(jnp.int32, (tiles, stretch), 1) // TILE
    tile_is = lax.broadcasted_iota(jnp.int32, (tiles, stretch), 0)
    for c in range(4):
        spread = (tile_is == tile_of + c * (stretch // TILE)).astype(f32).astype(bf16)
        keep[:, c * stretch : (c + 1) * stretch] = dot(supported, spread).astype(bf16)

    for c in range(groups):
        rows = slice(c * chunk, (c + 1) * chunk)
        for copy in bring(c):
            copy.wait()
        active = jnp.concatenate(visit_all(lambda row: foot_ref[row : row + BLOCK, rows]), axis=0) * keep[:, rows]
        act[:, rows] = active
        together = dot(active, active, NT)
        corr[...] = together if c == 0 else corr[...] + together
        loads = dot(active, frames_ref[rows, :])
        drive[...] = loads if c == 0 else drive[...] + loads

    line = lax.broadcasted_iota(jnp.int32, (three, three), 0)
    column = lax.broadcasted_iota(jnp.int32, (three, three), 1)
    on_diagonal = jnp.where(line == column, corr[...], 0.0)
    diag_out[...] = jnp.broadcast_to(jnp.sum(on_diagonal, axis=0, keepdims=True), diag_out.shape)
    own_diagonal = jnp.sum(on_diagonal, axis=1, keepdims=True)
    for offset in SIDES:
        start(send_diag, offset)

    sides, rest = slice(BLOCK, half), [slice(0, BLOCK), slice(half, three)]
    corr_sides = halves(corr[sides, :])
    corr_rest = halves(jnp.concatenate([corr[r, :] for r in rest], axis=0))
    def ordered(part, windows):
        blank = jnp.zeros((BLOCK, frames_here), bf16)
        return [visit(turn, w, traces_near[part, w, :BLOCK, :], traces_near[part, w, BLOCK:, :]) if w in windows else blank
                for turn in range(2) for w in WINDOWS]

    own_low = jnp.concatenate(ordered(1, (1,)), axis=0)
    for offset in SIDES:
        arrive(functools.partial(send_traces, 0), offset)
    high = jnp.concatenate(ordered(0, WINDOWS), axis=0)
    drive_high, drive_rest = halves(drive[sides, :] - product(corr_sides, (high, own_low)))
    drive_out[...] = drive_high
    for offset in SIDES:
        start(send_drive_high, offset)
    for turn in range(2):
        around[strip(turn, 1), :] = visit(turn, 1, traces_ref[:BLOCK, :], traces_ref[BLOCK:, :])
    for offset in SIDES:
        arrive(functools.partial(send_traces, 1), offset)
    low = jnp.concatenate(ordered(1, (0, 2)), axis=0)
    late_out[...] = (drive_rest.astype(f32) - dot(corr_sides[0], low)).astype(bf16)
    for offset in SIDES:
        start(send_late, offset)
    for turn in range(2):
        for window in (0, 2):
            row = place(turn, window)
            around[strip(turn, window), :] = high[row : row + BLOCK].astype(f32) + low[row : row + BLOCK].astype(f32)
    fitted = product(corr_rest, (high, own_low + low))
    drive[rest[0], :] -= fitted[:BLOCK]
    drive[rest[1], :] -= fitted[BLOCK:]
    ones = jnp.ones((8, frames_here), bf16)

    def level_of(rows):
        return (dot(ones, rows, NT) * (1.0 / frames_here)).astype(bf16)

    levels = []

    def foresee(rows):
        level = level_of(rows)
        for d in range(1, shares):
            beyond = pl.ds(first_of(partner(d), whole_rows), part_rows)
            guess[len(levels), d - 1] = dot(level, act[:, beyond])
        levels.append(level.astype(f32))

    foresee(high)

    for offset in SIDES:
        arrive(send_diag, offset)
    line = lax.broadcasted_iota(jnp.int32, (BLOCK, three), 0)
    column = lax.broadcasted_iota(jnp.int32, (BLOCK, three), 1)
    rates = []
    for turn in range(2):
        diagonal = own_diagonal[place(turn, 1) : place(turn, 1) + BLOCK]
        for offset in SIDES:
            theirs = jnp.where(column == line + place(turn, 1 - offset), diag_in[side(-offset), 0:1, :], 0.0)
            diagonal += jnp.sum(theirs, axis=1, keepdims=True)
        rates.append(1.0 / (diagonal + 1.0))

    before = [around[strip(turn, 1), :] for turn in range(2)]
    corr_late = halves(corr[half:, :half])
    for offset in SIDES:
        arrive(send_drive_high, offset)
    wanted = drive[strip(0, 1), :] + drive_in[0].astype(f32) + drive_in[1].astype(f32)
    for offset in SIDES:
        arrive(send_late, offset)
    wanted += late_in[0].astype(f32) + late_in[1].astype(f32)
    after_first = jnp.maximum(before[0] + wanted * rates[0], 0.0)
    near_first, rest_first = halves(after_first)
    near[strip(0, 1), :] = near_first
    for offset in SIDES:
        start(functools.partial(send_near, 0), offset)
    for d in range(1, shares):
        send_far(0, d).start()

    def total(rows):
        return jnp.sum(rows.astype(f32), axis=1, keepdims=True)

    def parts(band):
        known = near[bands[band], :]
        weight = total(known)
        for c, (begin, length) in enumerate(spans[band]):
            for d in range(1, shares):
                rows = pl.ds(first_of(partner(d), whole_rows + begin), length)
                part = dot(known, frames_ref[rows, :], NT) - weight * guess[(0, 1, 1, 2, 2, 2)[band], d - 1, 0:1, begin : begin + length]
                part_out[d - 1, bands[band], begin : begin + length] = part.astype(bf16)
                send_part(d, band, c).start()

    parts(0)
    rest_out[...] = rest_first
    for offset in SIDES:
        start(send_rest, offset)
    for offset in SIDES:
        start(send_drive, offset)
    foresee(jnp.concatenate([near_first, high[BLOCK:]], axis=0))

    arrive_mate(functools.partial(send_near, 0))
    parts(1)
    arrive_other(functools.partial(send_near, 0))
    for offset in SIDES:
        arrive(send_rest, offset)
    change = [after_first - before[0]]
    for window in (0, 2):
        there = near[strip(0, window), :].astype(f32) + rest_in[window // 2].astype(f32)
        change.append(there - around[strip(0, window), :])
    change = halves(jnp.concatenate(change, axis=0))
    extra[BLOCK:, :] = -product([x[BLOCK:] for x in corr_late], change)
    for offset in SIDES:
        start(send_extra, offset)
    parts(2)
    extra[:BLOCK, :] = -product([x[:BLOCK] for x in corr_late], change)
    foresee(jnp.concatenate([near[:half, :], high[half:]], axis=0))
    line = lax.broadcasted_iota(jnp.int32, (8, three), 0)
    hint_out[...] = jnp.where(line == 0, levels[0], jnp.where(line == 1, levels[1], levels[2]))
    for d in range(1, shares):
        send_hint(d).start()

    for d in range(1, shares):
        send_far(0, d).wait_recv()
        for offset in SIDES:
            start(functools.partial(relay, 0, d), offset)

    for offset in SIDES:
        arrive(send_drive, offset)
        arrive(send_extra, offset)
    wanted = drive[strip(1, 1), :] + side_drive[0] + side_drive[1] + extra[0:BLOCK, :] + extra_in[0] + extra_in[1]
    after_second = jnp.maximum(before[1] + wanted * rates[1], 0.0)
    near[strip(1, 1), :] = after_second.astype(bf16)
    for offset in SIDES:
        start(functools.partial(send_near, 1), offset)
    for d in range(1, shares):
        send_far(1, d).start()
    parts(3)
    for block in range(2):
        updated_out[block * BLOCK : (block + 1) * BLOCK, :] = visit(block, 1, after_first, after_second)
    arrive_mate(functools.partial(send_near, 1))
    parts(4)
    arrive_other(functools.partial(send_near, 1))
    parts(5)

    for d in range(1, shares):
        send_far(1, d).wait_recv()
        for offset in SIDES:
            start(functools.partial(relay, 1, d), offset)

    known = near[...]
    regions = [(begin, min(512, share_rows - begin)) for begin in range(whole_rows, share_rows, 512)]
    for begin, length in [(0, whole_rows)] + regions:
        mix[:, begin : begin + length] = dot(known, frames_ref[pl.ds(first_of(mine, begin), length), :], NT)

    for d in range(1, shares):
        for turn in range(2):
            for offset in SIDES:
                arrive(functools.partial(relay, turn, d), offset)
    gram = dot(known, known, NT)
    for d in range(1, shares):
        gram += dot(near_far[d - 1], near_far[d - 1], NT)
    line = lax.broadcasted_iota(jnp.int32, (three, three), 0)
    column = lax.broadcasted_iota(jnp.int32, (three, three), 1)
    scale = jnp.sum(jnp.where(line == column, gram, 0.0), axis=1, keepdims=True) + 1.0
    rate = 1.0 / scale
    grams = []
    for turn in range(2):
        high, low = halves(gram[turn * half : (turn + 1) * half])
        grams.append((jnp.concatenate([high, low], axis=0), high[:, :half]))

    def step_one(begin, length):
        here, cols = pl.ds(first_of(mine, begin), length), slice(begin, begin + length)
        active = act[:, here]
        fitted = dot(grams[0][0], active)
        left_over = mix[:half, cols] - fitted[:half] - fitted[half:]
        grown = active[:half].astype(f32) + left_over * rate[:half]
        after = jnp.maximum(grown, 0.0) * keep[:half, here].astype(f32)
        high, low = halves(after)
        shaped[:, cols] = high
        fitted = dot(grams[1][0], jnp.concatenate([high, active[half:]], axis=0))
        mix[half:, cols] += active[half:].astype(f32) * scale[half:] - fitted[:half] - fitted[half:] - dot(grams[1][1], low)

    def step_two(begin, length):
        here, cols = pl.ds(first_of(mine, begin), length), slice(begin, begin + length)
        after = jnp.maximum(mix[half:, cols] * rate[half:], 0.0) * keep[half:, here].astype(f32)
        second = after.astype(bf16)
        for window in range(3):
            row = place(0, window)
            for block in range(2):
                out = window * width + block * BLOCK
                refined_out[out : out + BLOCK, cols] = visit(
                    block, window, shaped[row : row + BLOCK, cols], second[row : row + BLOCK])

    for d in range(1, shares):
        for p in range(whole_pieces):
            send_frames(d, p).wait_recv()
        mix[:, :whole_rows] += dot(near_far[d - 1], frames_in[d - 1], NT)
    step_one(0, whole_rows)
    step_two(0, whole_rows)

    for d in range(1, shares):
        send_hint(d).wait_recv()
    weights = [total(near_far[d - 1]) for d in range(1, shares)]
    for d in range(1, shares):
        for band in range(3):
            for c in range(len(spans[band])):
                send_part(d, band, c).wait_recv()
    for begin, length in regions:
        here, cols = pl.ds(first_of(mine, begin), length), slice(begin, begin + length)
        for d in range(1, shares):
            guesses = dot(hint_in[d - 1].astype(bf16), act[:, here])
            near_part = part_in[d - 1, :half, begin - whole_rows : begin - whole_rows + length].astype(f32)
            weight = weights[d - 1]
            mix[:BLOCK, cols] += near_part[:BLOCK] + weight[:BLOCK] * guesses[0:1]
            mix[BLOCK:half, cols] += near_part[BLOCK:] + weight[BLOCK:half] * guesses[1:2]
            mix[half:, cols] += weight[half:] * guesses[2:3]
        step_one(begin, length)
    for offset in SIDES:
        for copy in (send_late, send_drive_high, send_drive, send_diag, send_rest, send_extra):
            left(copy, offset)
        for turn in range(2):
            left(functools.partial(send_traces, turn), offset)
            left(functools.partial(send_near, turn), offset)
            for d in range(1, shares):
                left(functools.partial(relay, turn, d), offset)
    for d in range(1, shares):
        send_hint(d).wait_send()
        for turn in range(2):
            send_far(turn, d).wait_send()
        for p in range(whole_pieces):
            send_frames(d, p).wait_send()
        for band in range(3):
            for c in range(len(spans[band])):
                send_part(d, band, c).wait_send()
    for d in range(1, shares):
        send_part(d, 3, 0).wait_recv()
        send_part(d, 4, 0).wait_recv()
    for c, (begin, length) in enumerate(spans[5]):
        cols = slice(whole_rows + begin, whole_rows + begin + length)
        for d in range(1, shares):
            send_part(d, 5, c).wait_recv()
            mix[half:, cols] += part_in[d - 1, half:, begin : begin + length].astype(f32)
        step_two(whole_rows + begin, length)
    for d in range(1, shares):
        for band in range(3, 6):
            for c in range(len(spans[band])):
                send_part(d, band, c).wait_send()


def deliver_kernel(refined_ref, updated_ref, refined_out, updated_out, sem):
    rows = refined_ref.shape[0] // 4
    moves = [(updated_ref, updated_out)]
    for i in range(4):
        part = pl.ds(i * rows, rows)
        moves.append((refined_ref.at[part], refined_out.at[part]))
    copies = [pltpu.make_async_copy(a, b, sem.at[i]) for i, (a, b) in enumerate(moves)]
    for copy in copies:
        copy.start()
    for copy in copies:
        copy.wait()


def deliver(refined, updated):
    refined, updated = (pltpu.with_memory_space_constraint(x, pltpu.VMEM) for x in (refined, updated))
    like = [jax.ShapeDtypeStruct(x.shape, x.dtype) for x in (refined, updated)]
    anywhere = pl.BlockSpec(memory_space=pl.ANY)
    refined, updated = pl.pallas_call(
        deliver_kernel, out_shape=like, in_specs=[anywhere] * 2, out_specs=[anywhere] * 2,
        scratch_shapes=[pltpu.SemaphoreType.DMA((5,))],
    )(refined, updated)
    return refined.T, updated


def cut(rows):
    early, late = (512, 256) if rows > 512 else (128, 128)
    front = [early, rows - early] if rows > early else [rows]
    back = [rows - late, late] if rows > late else [rows]
    return [front, [rows], [rows], [rows], [rows], back]


def shards(owners, shares, frames, footprints, support, traces, block_order):
    pixels, frames_here = frames.shape
    width = traces.shape[0]
    three = 3 * width
    share_rows = pixels // shares
    whole_rows = max(share_rows * WHOLE // 16 // 128, 1) * 128
    part_rows = share_rows - whole_rows
    chunks = cut(part_rows)
    others = shares - 1
    groups = 2
    vmem, dma = pltpu.VMEM, pltpu.SemaphoreType.DMA
    refined, updated = pl.pallas_call(
        functools.partial(kernel, owners, shares, chunks),
        out_shape=(pltpu.VMEM((three, share_rows), bf16), pltpu.VMEM(traces.shape, f32)),
        in_specs=[pl.BlockSpec(memory_space=pltpu.HBM)] * 5,
        out_specs=[pl.BlockSpec(memory_space=pltpu.VMEM)] * 2,
        scratch_shapes=[
            pltpu.SMEM(block_order.shape[::-1], jnp.int32),
            vmem(frames.shape, bf16),
            vmem((three, pixels), bf16),
            vmem(support.shape[::-1], jnp.int32),
            vmem(traces.shape, f32),
            vmem((2, 3) + traces.shape, bf16),
            vmem((2 * BLOCK, frames_here), bf16),
            vmem((2, BLOCK, frames_here), bf16),
            vmem((2 * BLOCK, frames_here), bf16),
            vmem((2, BLOCK, frames_here), bf16),
            vmem((three, pixels), bf16),
            vmem((three, pixels), bf16),
            vmem((three, frames_here), f32),
            vmem((three, frames_here), f32),
            vmem((three, three), f32),
            vmem((8, three), f32),
            vmem((2, 8, three), f32),
            vmem((2, BLOCK, frames_here), f32),
            vmem((BLOCK, frames_here), bf16),
            vmem((2, BLOCK, frames_here), bf16),
            vmem((3 * BLOCK, frames_here), f32),
            vmem((2, BLOCK, frames_here), f32),
            vmem((three, frames_here), bf16),
            vmem((others, three, frames_here), bf16),
            vmem((3, others, 8, part_rows), f32),
            vmem((8, three), f32),
            vmem((others, 8, three), f32),
            vmem((others, whole_rows, frames_here), bf16),
            vmem((others, three, part_rows), bf16),
            vmem((others, three, part_rows), bf16),
            vmem((three, share_rows), f32),
            vmem((three // 2, share_rows), bf16),
            dma((groups + 2, 2)),
            dma((2, 2)), dma((2, 2)), dma((2,)), dma((2,)), dma((2, 2)), dma((2, 2)),
            dma((2,)), dma((2,)), dma((2,)), dma((2,)), dma((2, 2)), dma((2, 2)),
            dma((others, 2)), dma((others, 2)), dma((others, 2, 2)), dma((others, 2, 2)),
            dma((others,)), dma((others,)),
            dma((others, 1)), dma((others, 1)),
            dma((others, 6, 2)), dma((others, 6, 2)), dma((2,)), dma((2,)),
        ],
        compiler_params=pltpu.CompilerParams(
            collective_id=0, has_side_effects=True, vmem_limit_bytes=56 * 1024 * 1024
        ),
    )(block_order.T, frames, footprints.T, support.T, traces)
    return deliver(refined, updated)


def solution(mesh):
    in_specs = (P("pix", "frm"), P("pix", None), P("pix", None), P("pix", "frm"), P())
    out_specs = (P(("pix", "frm"), None), P("pix", "frm"))
    body = functools.partial(shards, mesh.shape["pix"], mesh.shape["frm"])
    return jax.shard_map(body, mesh=mesh, in_specs=in_specs, out_specs=out_specs, check_vma=False)
```

```python
import functools

import jax
import jax.numpy as jnp
from jax import lax
from jax.experimental import pallas as pl
from jax.experimental.pallas import tpu as pltpu
from jax.sharding import PartitionSpec as P

BLOCK = 32
TILE = 16
MESH = pl.DeviceIdType.MESH
SIDES = (-1, 1)
WINDOWS = (1, 0, 2)
WHOLE = 3
f32, bf16 = jnp.float32, jnp.bfloat16
NT = ((1,), (1,))


def dot(a, b, dims=((1,), (0,))):
    return lax.dot_general(a, b, (dims, ((), ())), preferred_element_type=f32)


def halves(x):
    high = x.astype(bf16)
    return high, (x - high.astype(f32)).astype(bf16)


def place(turn, window):
    return (turn * 3 + WINDOWS.index(window)) * BLOCK


def strip(turn, window):
    return pl.ds(place(turn, window), BLOCK)


def product(a, b):
    (a_high, a_low), (high, low) = a, b
    both = dot(jnp.concatenate([a_high, a_low], axis=0), high)
    n = a_high.shape[0]
    return both[:n] + both[n:] + dot(a_high, low)


def kernel(
    owners, shares, chunks, order_hbm, frames_hbm, foot_hbm, support_hbm, traces_hbm, refined_out, updated_out,
    order_ref, frames_ref, foot_ref, support_ref, traces_ref, traces_near, late_out, late_in, drive_out, drive_in, act, keep, around, drive, corr, diag_out, diag_in, side_drive,
    rest_out, rest_in, extra, extra_in, near, near_far, guess, hint_out, hint_in, frames_in, part_out, part_in, mix, shaped,
    in_sem, a_send, a_recv, b_send, b_recv, c_send, c_recv, d_send, d_recv, e_send, e_recv, g_send, g_recv,
    h_send, h_recv, i_send, i_recv, j_send, j_recv, k_send, k_recv, l_send, l_recv, m_send, m_recv,
):
    slab, mine = lax.axis_index("pix"), lax.axis_index("frm")
    pixels, frames_here = frames_ref.shape
    three = act.shape[0]
    half = three // 2
    width = three // 3
    share_rows = pixels // shares
    whole_rows = frames_in.shape[1]
    part_rows = share_rows - whole_rows
    whole_pieces = k_send.shape[1]
    piece = whole_rows // whole_pieces
    spans = [[(sum(sizes[:i]), size) for i, size in enumerate(sizes)] for sizes in chunks]
    barrier = pltpu.get_barrier_semaphore()

    def present(offset):
        return slab > 0 if offset < 0 else slab < owners - 1

    def partner(d):
        return lax.rem(mine + d, shares)

    for offset in SIDES:
        @pl.when(present(offset))
        def _():
            pl.semaphore_signal(barrier, inc=1, device_id=(slab + offset, mine), device_id_type=MESH)
    for d in range(1, shares):
        pl.semaphore_signal(barrier, inc=1, device_id=(slab, partner(d)), device_id_type=MESH)

    groups = in_sem.shape[0] - 2
    chunk = pixels // groups

    def bring(c):
        rows = pl.ds(c * chunk, chunk)
        return [pltpu.make_async_copy(foot_hbm.at[:, rows], foot_ref.at[:, rows], in_sem.at[c, 0]),
                pltpu.make_async_copy(frames_hbm.at[rows], frames_ref.at[rows], in_sem.at[c, 1])]

    fetch_support = pltpu.make_async_copy(support_hbm, support_ref, in_sem.at[groups, 0])
    fetch_traces = pltpu.make_async_copy(traces_hbm, traces_ref, in_sem.at[groups, 1])
    fetch_order = pltpu.make_async_copy(order_hbm, order_ref, in_sem.at[groups + 1, 0])
    fetch_traces.start()
    fetch_support.start()
    fetch_order.start()
    for c in range(groups):
        for copy in bring(c):
            copy.start()

    def side(offset):
        return 1 if offset < 0 else 0

    for offset in SIDES:
        @pl.when(jnp.logical_not(present(offset)))
        def _():
            here = side(-offset)
            diag_in[here] = jnp.zeros(diag_in.shape[1:], f32)
            side_drive[here] = jnp.zeros(side_drive.shape[1:], f32)
            rest_in[here] = jnp.zeros(rest_in.shape[1:], bf16)
            extra_in[here] = jnp.zeros(extra_in.shape[1:], f32)
            drive_in[here] = jnp.zeros(drive_in.shape[1:], bf16)
            late_in[here] = jnp.zeros(late_in.shape[1:], bf16)
            for part in range(2):
                traces_near[part, 1 + offset] = jnp.zeros(traces_near.shape[2:], bf16)
            for turn in range(2):
                near[strip(turn, 1 + offset), :] = jnp.zeros((BLOCK, frames_here), bf16)
                for d in range(1, shares):
                    near_far[d - 1, strip(turn, 1 + offset), :] = jnp.zeros((BLOCK, frames_here), bf16)

    def remote(src, dst, send, recv, to):
        return pltpu.make_async_remote_copy(
            src_ref=src, dst_ref=dst, send_sem=send, recv_sem=recv, device_id=to, device_id_type=MESH)

    def beside(offset):
        return slab + offset, mine

    def send_traces(part, offset):
        s = side(offset)
        return remote(traces_near.at[part, 1], traces_near.at[part, 1 - offset], a_send.at[s, part], a_recv.at[s, part],
                      beside(offset))

    def send_late(offset):
        s = side(offset)
        return remote(late_out.at[pl.ds(place(0, 1 + offset) - BLOCK, BLOCK)], late_in.at[s], m_send.at[s], m_recv.at[s],
                      beside(offset))

    def send_diag(offset):
        s = side(offset)
        return remote(diag_out, diag_in.at[s], b_send.at[s], b_recv.at[s], beside(offset))

    def send_drive_high(offset):
        s = side(offset)
        return remote(drive_out.at[pl.ds(place(0, 1 + offset) - BLOCK, BLOCK)], drive_in.at[s], c_send.at[s, 0], c_recv.at[s, 0],
                      beside(offset))

    def send_drive(offset):
        s = side(offset)
        return remote(drive.at[strip(1, 1 + offset)], side_drive.at[s], c_send.at[s, 1], c_recv.at[s, 1], beside(offset))

    def send_rest(offset):
        s = side(offset)
        return remote(rest_out, rest_in.at[s], d_send.at[s], d_recv.at[s], beside(offset))

    def send_extra(offset):
        s = side(offset)
        return remote(extra.at[pl.ds(place(0, 1 + offset), BLOCK)], extra_in.at[s], e_send.at[s], e_recv.at[s], beside(offset))

    def send_near(turn, offset):
        s = side(offset)
        return remote(near.at[strip(turn, 1)], near.at[strip(turn, 1 - offset)], g_send.at[s, turn], g_recv.at[s, turn],
                      beside(offset))

    def send_far(turn, d):
        return remote(near.at[strip(turn, 1)], near_far.at[d - 1, strip(turn, 1)], h_send.at[d - 1, turn], h_recv.at[d - 1, turn],
                      (slab, partner(d)))

    def relay(turn, d, offset):
        s = side(offset)
        return remote(near_far.at[d - 1, strip(turn, 1)], near_far.at[d - 1, strip(turn, 1 - offset)],
                      i_send.at[d - 1, s, turn], i_recv.at[d - 1, s, turn], beside(offset))

    def send_hint(d):
        return remote(hint_out, hint_in.at[d - 1], j_send.at[d - 1], j_recv.at[d - 1], (slab, partner(d)))

    def first_of(who, row):
        return pl.multiple_of(who * share_rows + row, 128)

    def send_frames(d, p):
        return remote(frames_hbm.at[pl.ds(first_of(partner(d), p * piece), piece)], frames_in.at[d - 1, pl.ds(p * piece, piece)],
                      k_send.at[d - 1, p], k_recv.at[d - 1, p], (slab, partner(d)))

    mate = 1 - 2 * lax.rem(slab, 2)
    mate_row = pl.multiple_of((1 + (mate + 1) // 2) * BLOCK, BLOCK)
    other_row = pl.multiple_of((2 - (mate + 1) // 2) * BLOCK, BLOCK)
    bands = [pl.ds(turn * half + row, BLOCK) for turn in range(2) for row in (0, mate_row, other_row)]

    def send_part(d, band, c):
        where = (d - 1, bands[band], pl.ds(*spans[band][c]))
        return remote(part_out.at[where], part_in.at[where], l_send.at[d - 1, band, c], l_recv.at[d - 1, band, c], (slab, partner(d)))

    def start(copy, offset):
        @pl.when(present(offset))
        def _():
            copy(offset).start()

    def arrive(copy, offset):
        @pl.when(present(-offset))
        def _():
            copy(offset).wait_recv()

    def arrive_mate(copy):
        for offset in SIDES:
            @pl.when(jnp.logical_and(present(-offset), mate == -offset))
            def _():
                copy(offset).wait_recv()

    def arrive_other(copy):
        for offset in SIDES:
            @pl.when(jnp.logical_and(present(-offset), mate == offset))
            def _():
                copy(offset).wait_recv()

    def left(copy, offset):
        @pl.when(present(offset))
        def _():
            copy(offset).wait_send()

    def visited(turn, window):
        return order_ref[turn, jnp.clip(slab - 1 + window, 0, owners - 1)]

    def visit(turn, window, low, high):
        in_order = visited(0, window) == 0
        return jnp.where(in_order, low, high) if turn == 0 else jnp.where(in_order, high, low)

    def visit_all(load):
        pairs = {w: (load(w * width), load(w * width + BLOCK)) for w in WINDOWS}
        return [visit(turn, w, *pairs[w]) for turn in range(2) for w in WINDOWS]

    peers = present(-1).astype(jnp.int32) + present(1).astype(jnp.int32) + shares - 1
    pl.semaphore_wait(barrier, peers)
    for p in range(whole_pieces):
        for d in range(1, shares):
            send_frames(d, p).start()
    fetch_traces.wait()
    for part, value in enumerate(halves(traces_ref[...])):
        traces_near[part, 1] = value
        for offset in SIDES:
            start(functools.partial(send_traces, part), offset)

    usable = {0: (slab > 0).astype(f32), 1: 1.0, 2: (slab < owners - 1).astype(f32)}
    fetch_order.wait()
    fetch_support.wait()
    supported = jnp.concatenate(visit_all(
        lambda row: support_ref[row : row + BLOCK, :].astype(f32) * usable[row // width]), axis=0).astype(bf16)
    tiles = support_ref.shape[1]
    stretch = pixels // 4
    tile_of = lax.broadcasted_iota(jnp.int32, (tiles, stretch), 1) // TILE
    tile_is = lax.broadcasted_iota(jnp.int32, (tiles, stretch), 0)
    for c in range(4):
        spread = (tile_is == tile_of + c * (stretch // TILE)).astype(f32).astype(bf16)
        keep[:, c * stretch : (c + 1) * stretch] = dot(supported, spread).astype(bf16)

    for c in range(groups):
        rows = slice(c * chunk, (c + 1) * chunk)
        for copy in bring(c):
            copy.wait()
        active = jnp.concatenate(visit_all(lambda row: foot_ref[row : row + BLOCK, rows]), axis=0) * keep[:, rows]
        act[:, rows] = active
        together = dot(active, active, NT)
        corr[...] = together if c == 0 else corr[...] + together
        loads = dot(active, frames_ref[rows, :])
        drive[...] = loads if c == 0 else drive[...] + loads

    line = lax.broadcasted_iota(jnp.int32, (three, three), 0)
    column = lax.broadcasted_iota(jnp.int32, (three, three), 1)
    on_diagonal = jnp.where(line == column, corr[...], 0.0)
    diag_out[...] = jnp.broadcast_to(jnp.sum(on_diagonal, axis=0, keepdims=True), diag_out.shape)
    own_diagonal = jnp.sum(on_diagonal, axis=1, keepdims=True)
    for offset in SIDES:
        start(send_diag, offset)

    sides, rest = slice(BLOCK, half), [slice(0, BLOCK), slice(half, three)]
    corr_sides = halves(corr[sides, :])
    corr_rest = halves(jnp.concatenate([corr[r, :] for r in rest], axis=0))
    def ordered(part, windows):
        blank = jnp.zeros((BLOCK, frames_here), bf16)
        return [visit(turn, w, traces_near[part, w, :BLOCK, :], traces_near[part, w, BLOCK:, :]) if w in windows else blank
                for turn in range(2) for w in WINDOWS]

    own_low = jnp.concatenate(ordered(1, (1,)), axis=0)
    for offset in SIDES:
        arrive(functools.partial(send_traces, 0), offset)
    high = jnp.concatenate(ordered(0, WINDOWS), axis=0)
    drive_high, drive_rest = halves(drive[sides, :] - product(corr_sides, (high, own_low)))
    drive_out[...] = drive_high
    for offset in SIDES:
        start(send_drive_high, offset)
    for turn in range(2):
        around[strip(turn, 1), :] = visit(turn, 1, traces_ref[:BLOCK, :], traces_ref[BLOCK:, :])
    for offset in SIDES:
        arrive(functools.partial(send_traces, 1), offset)
    low = jnp.concatenate(ordered(1, (0, 2)), axis=0)
    late_out[...] = (drive_rest.astype(f32) - dot(corr_sides[0], low)).astype(bf16)
    for offset in SIDES:
        start(send_late, offset)
    for turn in range(2):
        for window in (0, 2):
            row = place(turn, window)
            around[strip(turn, window), :] = high[row : row + BLOCK].astype(f32) + low[row : row + BLOCK].astype(f32)
    fitted = product(corr_rest, (high, own_low + low))
    drive[rest[0], :] -= fitted[:BLOCK]
    drive[rest[1], :] -= fitted[BLOCK:]
    ones = jnp.ones((8, frames_here), bf16)

    def level_of(rows):
        return (dot(ones, rows, NT) * (1.0 / frames_here)).astype(bf16)

    levels = []

    def foresee(rows):
        level = level_of(rows)
        for d in range(1, shares):
            beyond = pl.ds(first_of(partner(d), whole_rows), part_rows)
            guess[len(levels), d - 1] = dot(level, act[:, beyond])
        levels.append(level.astype(f32))

    foresee(high)

    for offset in SIDES:
        arrive(send_diag, offset)
    line = lax.broadcasted_iota(jnp.int32, (BLOCK, three), 0)
    column = lax.broadcasted_iota(jnp.int32, (BLOCK, three), 1)
    rates = []
    for turn in range(2):
        diagonal = own_diagonal[place(turn, 1) : place(turn, 1) + BLOCK]
        for offset in SIDES:
            theirs = jnp.where(column == line + place(turn, 1 - offset), diag_in[side(-offset), 0:1, :], 0.0)
            diagonal += jnp.sum(theirs, axis=1, keepdims=True)
        rates.append(1.0 / (diagonal + 1.0))

    before = [around[strip(turn, 1), :] for turn in range(2)]
    corr_late = halves(corr[half:, :half])
    for offset in SIDES:
        arrive(send_drive_high, offset)
    wanted = drive[strip(0, 1), :] + drive_in[0].astype(f32) + drive_in[1].astype(f32)
    for offset in SIDES:
        arrive(send_late, offset)
    wanted += late_in[0].astype(f32) + late_in[1].astype(f32)
    after_first = jnp.maximum(before[0] + wanted * rates[0], 0.0)
    near_first, rest_first = halves(after_first)
    near[strip(0, 1), :] = near_first
    for offset in SIDES:
        start(functools.partial(send_near, 0), offset)
    for d in range(1, shares):
        send_far(0, d).start()

    def total(rows):
        return jnp.sum(rows.astype(f32), axis=1, keepdims=True)

    def parts(band):
        known = near[bands[band], :]
        weight = total(known)
        for c, (begin, length) in enumerate(spans[band]):
            for d in range(1, shares):
                rows = pl.ds(first_of(partner(d), whole_rows + begin), length)
                part = dot(known, frames_ref[rows, :], NT) - weight * guess[(0, 1, 1, 2, 2, 2)[band], d - 1, 0:1, begin : begin + length]
                part_out[d - 1, bands[band], begin : begin + length] = part.astype(bf16)
                send_part(d, band, c).start()

    parts(0)
    rest_out[...] = rest_first
    for offset in SIDES:
        start(send_rest, offset)
    for offset in SIDES:
        start(send_drive, offset)
    foresee(jnp.concatenate([near_first, high[BLOCK:]], axis=0))

    arrive_mate(functools.partial(send_near, 0))
    parts(1)
    arrive_other(functools.partial(send_near, 0))
    for offset in SIDES:
        arrive(send_rest, offset)
    change = [after_first - before[0]]
    for window in (0, 2):
        there = near[strip(0, window), :].astype(f32) + rest_in[window // 2].astype(f32)
        change.append(there - around[strip(0, window), :])
    change = halves(jnp.concatenate(change, axis=0))
    extra[BLOCK:, :] = -product([x[BLOCK:] for x in corr_late], change)
    for offset in SIDES:
        start(send_extra, offset)
    parts(2)
    extra[:BLOCK, :] = -product([x[:BLOCK] for x in corr_late], change)
    foresee(jnp.concatenate([near[:half, :], high[half:]], axis=0))
    line = lax.broadcasted_iota(jnp.int32, (8, three), 0)
    hint_out[...] = jnp.where(line == 0, levels[0], jnp.where(line == 1, levels[1], levels[2]))
    for d in range(1, shares):
        send_hint(d).start()

    for d in range(1, shares):
        send_far(0, d).wait_recv()
        for offset in SIDES:
            start(functools.partial(relay, 0, d), offset)

    for offset in SIDES:
        arrive(send_drive, offset)
        arrive(send_extra, offset)
    wanted = drive[strip(1, 1), :] + side_drive[0] + side_drive[1] + extra[0:BLOCK, :] + extra_in[0] + extra_in[1]
    after_second = jnp.maximum(before[1] + wanted * rates[1], 0.0)
    near[strip(1, 1), :] = after_second.astype(bf16)
    for offset in SIDES:
        start(functools.partial(send_near, 1), offset)
    for d in range(1, shares):
        send_far(1, d).start()
    parts(3)
    for block in range(2):
        updated_out[block * BLOCK : (block + 1) * BLOCK, :] = visit(block, 1, after_first, after_second)
    arrive_mate(functools.partial(send_near, 1))
    parts(4)
    arrive_other(functools.partial(send_near, 1))
    parts(5)

    for d in range(1, shares):
        send_far(1, d).wait_recv()
        for offset in SIDES:
            start(functools.partial(relay, 1, d), offset)

    known = near[...]
    regions = [(begin, min(512, share_rows - begin)) for begin in range(whole_rows, share_rows, 512)]
    for begin, length in [(0, whole_rows)] + regions:
        mix[:, begin : begin + length] = dot(known, frames_ref[pl.ds(first_of(mine, begin), length), :], NT)

    for d in range(1, shares):
        for turn in range(2):
            for offset in SIDES:
                arrive(functools.partial(relay, turn, d), offset)
    gram = dot(known, known, NT)
    for d in range(1, shares):
        gram += dot(near_far[d - 1], near_far[d - 1], NT)
    line = lax.broadcasted_iota(jnp.int32, (three, three), 0)
    column = lax.broadcasted_iota(jnp.int32, (three, three), 1)
    scale = jnp.sum(jnp.where(line == column, gram, 0.0), axis=1, keepdims=True) + 1.0
    rate = 1.0 / scale
    grams = []
    for turn in range(2):
        high, low = halves(gram[turn * half : (turn + 1) * half])
        grams.append((jnp.concatenate([high, low], axis=0), high[:, :half]))

    def step_one(begin, length):
        here, cols = pl.ds(first_of(mine, begin), length), slice(begin, begin + length)
        active = act[:, here]
        fitted = dot(grams[0][0], active)
        left_over = mix[:half, cols] - fitted[:half] - fitted[half:]
        grown = active[:half].astype(f32) + left_over * rate[:half]
        after = jnp.maximum(grown, 0.0) * keep[:half, here].astype(f32)
        high, low = halves(after)
        shaped[:, cols] = high
        fitted = dot(grams[1][0], jnp.concatenate([high, active[half:]], axis=0))
        mix[half:, cols] += active[half:].astype(f32) * scale[half:] - fitted[:half] - fitted[half:] - dot(grams[1][1], low)

    def step_two(begin, length):
        here, cols = pl.ds(first_of(mine, begin), length), slice(begin, begin + length)
        after = jnp.maximum(mix[half:, cols] * rate[half:], 0.0) * keep[half:, here].astype(f32)
        second = after.astype(bf16)
        for window in range(3):
            row = place(0, window)
            for block in range(2):
                out = window * width + block * BLOCK
                refined_out[out : out + BLOCK, cols] = visit(
                    block, window, shaped[row : row + BLOCK, cols], second[row : row + BLOCK])

    for d in range(1, shares):
        for p in range(whole_pieces):
            send_frames(d, p).wait_recv()
        mix[:, :whole_rows] += dot(near_far[d - 1], frames_in[d - 1], NT)
    step_one(0, whole_rows)
    step_two(0, whole_rows)

    for d in range(1, shares):
        send_hint(d).wait_recv()
    weights = [total(near_far[d - 1]) for d in range(1, shares)]
    for d in range(1, shares):
        for band in range(3):
            for c in range(len(spans[band])):
                send_part(d, band, c).wait_recv()
    for begin, length in regions:
        here, cols = pl.ds(first_of(mine, begin), length), slice(begin, begin + length)
        for d in range(1, shares):
            guesses = dot(hint_in[d - 1].astype(bf16), act[:, here])
            near_part = part_in[d - 1, :half, begin - whole_rows : begin - whole_rows + length].astype(f32)
            weight = weights[d - 1]
            mix[:BLOCK, cols] += near_part[:BLOCK] + weight[:BLOCK] * guesses[0:1]
            mix[BLOCK:half, cols] += near_part[BLOCK:] + weight[BLOCK:half] * guesses[1:2]
            mix[half:, cols] += weight[half:] * guesses[2:3]
        step_one(begin, length)
    for offset in SIDES:
        for copy in (send_late, send_drive_high, send_drive, send_diag, send_rest, send_extra):
            left(copy, offset)
        for turn in range(2):
            left(functools.partial(send_traces, turn), offset)
            left(functools.partial(send_near, turn), offset)
            for d in range(1, shares):
                left(functools.partial(relay, turn, d), offset)
    for d in range(1, shares):
        send_hint(d).wait_send()
        for turn in range(2):
            send_far(turn, d).wait_send()
        for p in range(whole_pieces):
            send_frames(d, p).wait_send()
        for band in range(3):
            for c in range(len(spans[band])):
                send_part(d, band, c).wait_send()
    for d in range(1, shares):
        send_part(d, 3, 0).wait_recv()
        send_part(d, 4, 0).wait_recv()
    for c, (begin, length) in enumerate(spans[5]):
        cols = slice(whole_rows + begin, whole_rows + begin + length)
        for d in range(1, shares):
            send_part(d, 5, c).wait_recv()
            mix[half:, cols] += part_in[d - 1, half:, begin : begin + length].astype(f32)
        step_two(whole_rows + begin, length)
    for d in range(1, shares):
        for band in range(3, 6):
            for c in range(len(spans[band])):
                send_part(d, band, c).wait_send()


def deliver_kernel(refined_ref, updated_ref, refined_out, updated_out, sem):
    rows = refined_ref.shape[0] // 4
    moves = [(updated_ref, updated_out)]
    for i in range(4):
        part = pl.ds(i * rows, rows)
        moves.append((refined_ref.at[part], refined_out.at[part]))
    copies = [pltpu.make_async_copy(a, b, sem.at[i]) for i, (a, b) in enumerate(moves)]
    for copy in copies:
        copy.start()
    for copy in copies:
        copy.wait()


def deliver(refined, updated):
    refined, updated = (pltpu.with_memory_space_constraint(x, pltpu.VMEM) for x in (refined, updated))
    like = [jax.ShapeDtypeStruct(x.shape, x.dtype) for x in (refined, updated)]
    anywhere = pl.BlockSpec(memory_space=pl.ANY)
    refined, updated = pl.pallas_call(
        deliver_kernel, out_shape=like, in_specs=[anywhere] * 2, out_specs=[anywhere] * 2,
        scratch_shapes=[pltpu.SemaphoreType.DMA((5,))],
    )(refined, updated)
    return refined.T, updated


def cut(rows):
    early, late = (512, 256) if rows > 512 else (128, 128)
    front = [early, rows - early] if rows > early else [rows]
    back = [rows - late, late] if rows > late else [rows]
    return [front, [rows], [rows], [rows], [rows], back]


def shards(owners, shares, frames, footprints, support, traces, block_order):
    pixels, frames_here = frames.shape
    width = traces.shape[0]
    three = 3 * width
    share_rows = pixels // shares
    whole_rows = max(share_rows * WHOLE // 16 // 128, 1) * 128
    part_rows = share_rows - whole_rows
    chunks = cut(part_rows)
    others = shares - 1
    groups = 1
    vmem, dma = pltpu.VMEM, pltpu.SemaphoreType.DMA
    refined, updated = pl.pallas_call(
        functools.partial(kernel, owners, shares, chunks),
        out_shape=(pltpu.VMEM((three, share_rows), bf16), pltpu.VMEM(traces.shape, f32)),
        in_specs=[pl.BlockSpec(memory_space=pltpu.HBM)] * 5,
        out_specs=[pl.BlockSpec(memory_space=pltpu.VMEM)] * 2,
        scratch_shapes=[
            pltpu.SMEM(block_order.shape[::-1], jnp.int32),
            vmem(frames.shape, bf16),
            vmem((three, pixels), bf16),
            vmem(support.shape[::-1], jnp.int32),
            vmem(traces.shape, f32),
            vmem((2, 3) + traces.shape, bf16),
            vmem((2 * BLOCK, frames_here), bf16),
            vmem((2, BLOCK, frames_here), bf16),
            vmem((2 * BLOCK, frames_here), bf16),
            vmem((2, BLOCK, frames_here), bf16),
            vmem((three, pixels), bf16),
            vmem((three, pixels), bf16),
            vmem((three, frames_here), f32),
            vmem((three, frames_here), f32),
            vmem((three, three), f32),
            vmem((8, three), f32),
            vmem((2, 8, three), f32),
            vmem((2, BLOCK, frames_here), f32),
            vmem((BLOCK, frames_here), bf16),
            vmem((2, BLOCK, frames_here), bf16),
            vmem((3 * BLOCK, frames_here), f32),
            vmem((2, BLOCK, frames_here), f32),
            vmem((three, frames_here), bf16),
            vmem((others, three, frames_here), bf16),
            vmem((3, others, 8, part_rows), f32),
            vmem((8, three), f32),
            vmem((others, 8, three), f32),
            vmem((others, whole_rows, frames_here), bf16),
            vmem((others, three, part_rows), bf16),
            vmem((others, three, part_rows), bf16),
            vmem((three, share_rows), f32),
            vmem((three // 2, share_rows), bf16),
            dma((groups + 2, 2)),
            dma((2, 2)), dma((2, 2)), dma((2,)), dma((2,)), dma((2, 2)), dma((2, 2)),
            dma((2,)), dma((2,)), dma((2,)), dma((2,)), dma((2, 2)), dma((2, 2)),
            dma((others, 2)), dma((others, 2)), dma((others, 2, 2)), dma((others, 2, 2)),
            dma((others,)), dma((others,)),
            dma((others, 1)), dma((others, 1)),
            dma((others, 6, 2)), dma((others, 6, 2)), dma((2,)), dma((2,)),
        ],
        compiler_params=pltpu.CompilerParams(
            collective_id=0, has_side_effects=True, vmem_limit_bytes=56 * 1024 * 1024
        ),
    )(block_order.T, frames, footprints.T, support.T, traces)
    return deliver(refined, updated)


def solution(mesh):
    in_specs = (P("pix", "frm"), P("pix", None), P("pix", None), P("pix", "frm"), P())
    out_specs = (P(("pix", "frm"), None), P("pix", "frm"))
    body = functools.partial(shards, mesh.shape["pix"], mesh.shape["frm"])
    return jax.shard_map(body, mesh=mesh, in_specs=in_specs, out_specs=out_specs, check_vma=False)
```
